256 devices in a mesh: section: 8 (over y_hi, x), seq: 32 (over z, y_lo, core).
Axes of the slice: x: 4, y: 4 (y_hi: 2, y_lo: 2; y = y_hi * 2 + y_lo), z: 8, core: 2. Of those that a mesh axis runs over, the one named last changes fastest.
Arguments:
- features: bfloat16 [4096, 8192], P('seq', 'section'), may hold values from -600 to 600
- norm_gain: float32 [8192], P('section'), may hold values from 0.1 to 1.9
- kv_weight: bfloat16 [8192, 2048], P('section'), may hold values from -0.09375 to 0.09375
- queries: bfloat16 [3, 64, 4096, 128], P(None, 'section', 'seq'), may hold values from -64 to 64
- step_kv: bfloat16 [3, 8, 4096, 256], P(None, 'section', 'seq'), may hold values from -6 to 6
- doc_ids: int32 [4096], replicated, may hold values from 0 to 7, never falling along the last dimension, each value on 1 to 3072 neighbouring positions
- block_lists: int32 [3, 64, 16], replicated, may hold values from 0 to 63, as said below
Outputs:
- attended: bfloat16 [3, 64, 4096, 128], P(None, 'section', 'seq')
- kv_cache: bfloat16 [8, 4096, 256], P('section', 'seq')
The draws below stay inside these ranges and needn't reach their ends.
Inputs may be any that keep to these rules, and one draw needn't show every extreme that they name: `doc_ids`: document numbers never fall along the tokens; a document holds 1 to 3072 tokens, and one holds exactly 3072. `block_lists`: entry [k, b, 0] is b itself; every entry of row b is at most b; entries may repeat.
All inputs are finite; a program needn't handle non-finite values.
Results may differ from the reference program's by a relative error of at most 0.0084.
Values may be sent and summed in bfloat16 or wider, within the bound.
No kernel may reach another device: no remote copies, remote signals or barrier semaphores. Data moves between devices by JAX's collectives and lax.ppermute only.
A program may use at most 128 MiB of HBM per device.

```python
import math
import jax
import jax.numpy as jnp
import numpy as np
from jax import lax

D = 8192
HEADS = 64
KV_HEADS = 8
HEAD_DIM = 128
STEPS = 3
BLOCK = 64
LIST = 16
DOCS = 8
TOKENS = 4096
DOC_MOST = 3072


def step_values(key):
    folded = jax.random.fold_in(key, 11)
    array_shape = (STEPS, KV_HEADS, TOKENS, 2 * HEAD_DIM)
    sampled = jnp.clip(jax.random.normal(folded, array_shape, jnp.float32), -6.0, 6.0)
    return sampled


def draw_step_kv(key, part):
    return step_values(key).astype(jnp.bfloat16)


def draw_queries(key, part):
    array_shape = (STEPS, HEADS, TOKENS, HEAD_DIM)
    sampled = jnp.clip(jax.random.normal(jax.random.fold_in(key, 13), array_shape, jnp.float32), -6.0, 6.0)
    result = sampled
    return result.astype(jnp.bfloat16)


def draw_features(key, part):
    column_place = jnp.arange(D, dtype=jnp.float32)[None, :] / D
    sampled = jnp.clip(jax.random.normal(jax.random.fold_in(key, 31), (TOKENS, D), jnp.float32), -4.0, 4.0)
    token_scale = 10.0 ** jax.random.uniform(jax.random.fold_in(key, 37), (TOKENS, 1), jnp.float32)
    column_scale = 10.0 ** (0.477 * column_place + 0.523 * jax.random.uniform(jax.random.fold_in(key, 41), (1, D), jnp.float32))
    return (sampled * token_scale * column_scale).astype(jnp.bfloat16)


def draw_block_lists(key, part):
    blocks = TOKENS // BLOCK
    own_block = jnp.arange(blocks, dtype=jnp.int32)[None, :, None]
    raw_draws = jax.random.randint(jax.random.fold_in(key, 23), (STEPS, blocks, LIST), 0, 1 << 20)
    candidates = raw_draws % (own_block + 1)
    slot_index = jnp.arange(LIST, dtype=jnp.int32)[None, None, :]
    return jnp.where(slot_index == 0, own_block, candidates).astype(jnp.int32)


def spiked(values, own_key, source, target, shards_of, factor):
    owner, partner = [(jnp.arange(values.shape[position]) // (values.shape[position] // shards_of)).reshape([-1 if axis == position else 1 for axis in range(values.ndim)]) for position in (source, target)]
    chosen = jax.random.permutation(own_key, shards_of)[partner]
    strong = (owner == chosen) | (owner == (partner + shards_of // 2) % shards_of)
    return jnp.where(strong, factor * values, values)


def block_scale(own_key, dims, shards, least, largest):
    gain = 1.0
    for dim, shards_of in shards:
        steps = jax.random.uniform(jax.random.fold_in(jax.random.fold_in(own_key, 6), dim), (shards_of,), jnp.float32, least / len(shards), largest / len(shards))
        gain = gain * jnp.repeat(jnp.exp(steps), dims[dim] // shards_of).reshape((-1,) + (1,) * (len(dims) - 1 - dim))
    return gain


def length_profile(number_of, total, reach, slope):
    loads = [(1 << 20) // math.isqrt(rank ** slope) + 1 for rank in range(2, number_of + 1)]
    spare, counts = total - reach - (number_of - 1), [1] * (number_of - 1)
    while spare > 0:
        free = [i for i in range(number_of - 1) if counts[i] < reach]
        mass, remaining = sum([loads[i] for i in free]), spare
        for i in free:
            extra = min(reach - counts[i], max(1, remaining * loads[i] // mass), spare)
            counts[i] = counts[i] + extra
            spare = spare - extra
    return np.array([reach] + counts)


def ragged(key, number_of, total, reach, skew):
    if number_of == 2:
        one = jax.random.randint(key, (), max(1, total - reach), min(reach, total - 1) + 1)
        return jnp.stack([one, total - one])
    lengths = jnp.asarray(length_profile(number_of, total, reach, skew), jnp.int32)
    couples = (number_of - 1) // 2
    source_of, taker = lengths[1:1 + 2 * couples:2], lengths[2:2 + 2 * couples:2]
    room = jnp.minimum(source_of - 1, reach - taker)
    shifted = jax.random.randint(jax.random.fold_in(key, 1), (couples,), 0, 1 << 20) % (room + 1)
    lengths = lengths.at[1:1 + 2 * couples:2].set(source_of - shifted).at[2:2 + 2 * couples:2].set(taker + shifted)
    return lengths[jax.random.permutation(jax.random.fold_in(key, 2), number_of)]


def bell_draw_with(own_key, shape, deviation, limit, pieces, heavy, kind=jnp.bfloat16):
    values = deviation * jax.random.normal(own_key, shape, jnp.float32)
    if pieces:
        values = values * block_scale(own_key, shape, pieces, -0.22, 0.18)
    return jnp.clip(spiked(values, jax.random.fold_in(own_key, 3), *heavy), -limit, limit).astype(kind)


def setup_inputs(seed: int = 0) -> dict:
    splits = jax.random.split(jax.random.key(seed), 8)
    return {
        "features": draw_features(jax.random.fold_in(splits[7], 71), 0),
        "norm_gain": jnp.clip(1.0 + 0.18 * jax.random.normal(splits[1], (D,), jnp.float32), 0.1, 1.9),
        "kv_weight": bell_draw_with(splits[2], (D, KV_HEADS * 2 * HEAD_DIM), D ** -0.5, 0.09375, ((0, 8),), (0, 1, 8, 2.0)),
        "queries": draw_queries(jax.random.fold_in(splits[7], 71), 0),
        "step_kv": draw_step_kv(jax.random.fold_in(splits[7], 71), 0),
        "doc_ids": jnp.searchsorted(jnp.cumsum(ragged(splits[5], DOCS, TOKENS, DOC_MOST, 2)), jnp.arange(TOKENS), side="right").astype(jnp.int32),
        "block_lists": draw_block_lists(jax.random.fold_in(splits[7], 71), 0),
    }


neg_fill = -1e+30

def reference(features, norm_gain, kv_weight, queries, step_kv, doc_ids, block_lists):
    floated = features.astype(jnp.float32)
    inverse = lax.rsqrt(lax.optimization_barrier(jnp.mean(floated * floated, axis=1, keepdims=True)) + 1e-05)
    normalized = (floated * inverse * norm_gain[None, :]).astype(jnp.bfloat16)
    weight_heads = kv_weight.reshape(D, KV_HEADS, 2 * HEAD_DIM)
    kv_cache = jnp.einsum('td,dgc->gtc', normalized.astype(jnp.float32), weight_heads.astype(jnp.float32)).astype(jnp.bfloat16)
    blocks = TOKENS // BLOCK
    group_size = HEADS // KV_HEADS
    row_span = min(512, TOKENS)
    inv_sqrt = 1.0 / math.sqrt(HEAD_DIM)
    listed = jnp.any(block_lists[..., None] == jnp.arange(blocks, dtype=jnp.int32), axis=2)
    listed_tokens = jnp.repeat(listed, BLOCK, axis=2)
    positions = jnp.arange(TOKENS, dtype=jnp.int32)
    keys_all = kv_cache[..., :HEAD_DIM].astype(jnp.float32)
    values_all = kv_cache[..., HEAD_DIM:].astype(jnp.float32)
    step_index = jnp.arange(STEPS, dtype=jnp.int32)
    own_mask = (step_index[None, :] <= step_index[:, None])[:, None, None, :]

    def one_block(block_index):
        anchor = block_index * row_span
        row_pos = anchor + jnp.arange(row_span, dtype=jnp.int32)
        row_docs = lax.dynamic_slice_in_dim(doc_ids, anchor, row_span, 0)
        row_listed = lax.dynamic_slice_in_dim(listed_tokens, anchor // BLOCK, row_span // BLOCK, 1)
        row_listed = jnp.repeat(row_listed, BLOCK, axis=1)
        allowed = row_listed & (positions[None, None, :] <= row_pos[None, :, None]) & (doc_ids[None, None, :] == row_docs[None, :, None])
        query_rows = lax.dynamic_slice_in_dim(queries, anchor, row_span, 2).astype(jnp.float32)
        grouped = jnp.moveaxis(query_rows.reshape(STEPS, KV_HEADS, group_size, row_span, HEAD_DIM), 1, 0)
        step_rows = jnp.moveaxis(lax.dynamic_slice_in_dim(step_kv, anchor, row_span, 2).astype(jnp.float32), 1, 0)

        def one_head(operands):
            head_queries, head_keys, head_values, own_rows = operands
            own_keys = own_rows[..., :HEAD_DIM]
            own_values = own_rows[..., HEAD_DIM:]
            scores = jnp.einsum('sgrd,td->sgrt', head_queries, head_keys) * inv_sqrt
            own_scores = jnp.einsum('sgrd,mrd->sgrm', head_queries, own_keys) * inv_sqrt
            visible = allowed[:, None]
            run_max = jnp.maximum(lax.optimization_barrier(jnp.max(jnp.where(visible, scores, neg_fill), axis=-1)), lax.optimization_barrier(jnp.max(jnp.where(own_mask, own_scores, neg_fill), axis=-1)))
            weights = jnp.where(visible, jnp.exp(scores - run_max[..., None]), 0.0)
            own_weights = jnp.where(own_mask, jnp.exp(own_scores - run_max[..., None]), 0.0)
            run_sum = lax.optimization_barrier(jnp.sum(weights, axis=-1)) + lax.optimization_barrier(jnp.sum(own_weights, axis=-1))
            rounded = lax.optimization_barrier(weights.astype(jnp.bfloat16)).astype(jnp.float32)
            own_rounded = lax.optimization_barrier(own_weights.astype(jnp.bfloat16)).astype(jnp.float32)
            summed = jnp.einsum('sgrt,td->sgrd', rounded, head_values) + jnp.einsum('sgrm,mrd->sgrd', own_rounded, own_values)
            return (summed / run_sum[..., None]).astype(jnp.bfloat16)
        outputs = lax.map(one_head, (grouped, keys_all, values_all, step_rows))
        return jnp.moveaxis(outputs, 0, 1).reshape(STEPS, HEADS, row_span, HEAD_DIM)
    stacked = lax.map(one_block, jnp.arange(TOKENS // row_span, dtype=jnp.int32))
    attended = jnp.moveaxis(stacked, 0, 2).reshape(STEPS, HEADS, TOKENS, HEAD_DIM)
    return (attended, kv_cache)
```

```python
import functools
import math

import jax
import jax.numpy as jnp
from jax import lax
from jax.experimental import pallas as pl
from jax.experimental.pallas import tpu as pltpu
from jax.sharding import PartitionSpec as P

HEAD = 128
BLK = 64
LIST = 16
DOCS = 8
HIDDEN = -1e30
FAR = 1 << 24
EXTRA = 8
PAIR = 256
SLOTS = 7
LINE = 128
SIZES = (8, 12, 16)

VMEM_ALL = 60 << 20


def project_kernel(feat, gain, weight, out, scaled, tail):
    tokens = feat.shape[0]

    @pl.when(pl.program_id(0) == 0)
    def _():
        x = feat[...].astype(jnp.float32)
        g = x * gain[...]
        high = g.astype(jnp.bfloat16)
        scaled[:tokens] = high
        scaled[tokens:] = (g - high.astype(jnp.float32)).astype(jnp.bfloat16)
        total = jnp.sum(x * x, axis=1, keepdims=True)
        row = jnp.broadcast_to(total, (tokens, 128)).T[:EXTRA]
        top = row.astype(jnp.bfloat16).astype(jnp.float32)
        which = lax.broadcasted_iota(jnp.int32, (EXTRA, 128), 0)
        tail[...] = jnp.where(which == 0, top, jnp.where(which == 1, row - top, 0.0)).astype(jnp.bfloat16)

    product = jnp.dot(scaled[...], weight[...], preferred_element_type=jnp.float32)
    product = (product[:tokens] + product[tokens:]).astype(jnp.bfloat16)
    cols = out.shape[2]
    for j in range(out.shape[0]):
        out[j, :tokens, :] = product[:, j * cols : (j + 1) * cols]
        out[j, tokens:, :128] = tail[...]
        out[j, tokens:, 128:] = jnp.zeros_like(tail)


def project(features, norm_gain, kv_weight, heads):
    tokens, width = features.shape
    cols = kv_weight.shape[1] // heads
    grid = 2
    return pl.pallas_call(
        project_kernel,
        grid=(grid,),
        in_specs=[
            pl.BlockSpec((tokens, width), lambda i: (0, 0)),
            pl.BlockSpec((1, width), lambda i: (0, 0)),
            pl.BlockSpec((width, kv_weight.shape[1] // grid), lambda i: (0, i)),
        ],
        out_specs=pl.BlockSpec((heads // grid, tokens + EXTRA, cols), lambda i: (i, 0, 0)),
        out_shape=jax.ShapeDtypeStruct((heads, tokens + EXTRA, cols), jnp.bfloat16),
        scratch_shapes=[
            pltpu.VMEM((2 * tokens, width), jnp.bfloat16),
            pltpu.VMEM((EXTRA, 128), jnp.bfloat16),
        ],
        compiler_params=pltpu.CompilerParams(vmem_limit_bytes=VMEM_ALL),
        name="project",
    )(features, norm_gain.reshape(1, width), kv_weight)


def reduce_kernel(width, parts, out):
    tokens = out.shape[0]
    total = jnp.sum(parts[:, tokens:, :128].astype(jnp.float32), axis=0)
    squares = jnp.broadcast_to(total[0:1] + total[1:2], (128, tokens)).T
    inverse = lax.rsqrt(squares / width + 1e-05)
    for half in range(2):
        cols = slice(half * 128, half * 128 + 128)
        kept = parts[0, :tokens, cols].astype(jnp.float32)
        for s in range(1, parts.shape[0]):
            kept = kept + parts[s, :tokens, cols].astype(jnp.float32)
        out[:, cols] = (kept * inverse).astype(jnp.bfloat16)


def prepare_kernel(blocks_dev, place, lists, docs, table, seen):
    t = place[0]
    z = t // 4
    low = lax.rem(t, 4)
    units = lists.shape[0]
    d = docs[...]
    starts = [0] + [jnp.sum((d < doc).astype(jnp.int32)) for doc in range(1, DOCS)]
    for doc in range(DOCS):
        table[units * LINE + doc] = starts[doc]
    for c in range(seen.shape[0]):
        seen[c] = -1

    def unit_lists(u, carry):
        block = t * blocks_dev + lax.rem(u, blocks_dev)
        first = block * BLK
        begin = 0
        for doc in range(1, DOCS):
            begin = jnp.where(starts[doc] <= first, starts[doc], begin)
        least = begin // BLK
        for e in range(LIST):
            table[u * LINE + e] = 0
            table[u * LINE + 32 + e] = FAR
        n = 0
        for e in range(LIST):
            c = lists[u, e]
            keep = (c >= least) & (seen[c] != u)
            seen[c] = u
            away = lax.rem(c // 8 - z + 8, 8)
            slot = 0
            for a, s in ((7, 1), (6, 2), (2, 3), (5, 4), (3, 5), (4, 6)):
                slot = jnp.where(away == a, s, slot)
            x = lax.rem(c // 2, 4) ^ low
            row = ((x & 1) * SLOTS + slot) * PAIR + (x >> 1) * (2 * BLK) + lax.rem(c, 2) * BLK
            table[u * LINE + n] = row
            table[u * LINE + 32 + n] = jnp.where(keep, c * BLK, FAR)
            n = n + keep.astype(jnp.int32)
        table[u * LINE + 64] = n
        return carry

    lax.fori_loop(0, units, unit_lists, 0)


def attend_unit(blocks, u, k, half, block, begins, table, queries, own, held):
    last = (((1,), (1,)), ((), ()))
    first = (((0,), (0,)), ((), ()))
    scale = math.log2(math.e) / math.sqrt(HEAD)
    steps = own.shape[0]
    mine = pl.ds(pl.multiple_of(half * BLK, BLK), BLK)
    pieces = [held[pl.ds(pl.multiple_of(table[u * LINE + e], BLK), BLK), :] for e in range(blocks)]
    pieces += [own[m, 0, mine, :] for m in range(steps)]
    kv = jnp.concatenate(pieces, axis=0)
    lane = lax.rem(lax.broadcasted_iota(jnp.int32, (1, 128), 1), BLK)
    sub = lax.broadcasted_iota(jnp.int32, (BLK, 128), 0)
    pos_i = block * BLK + lane
    masks = []
    for e in range(blocks):
        pos_j = table[u * LINE + 32 + e] + sub
        masks.append((pos_j >= begins) & (pos_j <= pos_i))
    for m in range(steps):
        masks.append((sub == lane) & (m <= k))
    mask = jnp.concatenate(masks, axis=0)
    mask = jnp.concatenate([mask] * (queries.shape[0] // 128), axis=1)
    s = lax.dot_general(kv[:, :HEAD], queries, last, preferred_element_type=jnp.float32)
    s = jnp.where(mask, s, HIDDEN)
    top = jnp.max(s, axis=0, keepdims=True)
    p = jnp.exp2((s - top) * scale)
    total = jnp.sum(p, axis=0, keepdims=True)
    summed = lax.dot_general(kv[:, HEAD:], p.astype(jnp.bfloat16), first, preferred_element_type=jnp.float32)
    return (summed / total).T.astype(jnp.bfloat16)


def attend_kernel(blocks_dev, count, place, table, q, own, *refs):
    parts, (out, held, result, sems) = refs[:count], refs[count:]
    t = place[0]
    steps, heads, tokens, head_dim = q.shape
    units = steps * blocks_dev
    row = 0
    for part in parts:
        held[row : row + part.shape[0]] = part[...]
        row += part.shape[0]

    def copy(u):
        rows = pl.ds(pl.multiple_of(lax.rem(u, blocks_dev) * BLK, BLK), BLK)
        return pltpu.make_async_copy(result.at[u], out.at[u // blocks_dev, :, rows, :], sems.at[u])

    def unit_body(u, carry):
        k = u // blocks_dev
        half = lax.rem(u, blocks_dev)
        block = t * blocks_dev + half
        queries = q[k, :, pl.ds(pl.multiple_of(half * BLK, BLK), BLK), :].reshape(heads * BLK, head_dim)
        pos_i = block * BLK + lax.rem(lax.broadcasted_iota(jnp.int32, (1, 128), 1), BLK)
        begins = jnp.zeros((1, 128), jnp.int32)
        for doc in range(1, DOCS):
            start = table[units * LINE + doc]
            begins = jnp.where(start <= pos_i, start, begins)
        n = table[u * LINE + 64]
        least = 0
        for size in SIZES:

            @pl.when((n > least) & (n <= size))
            def _(size=size):
                value = attend_unit(size, u, k, half, block, begins, table, queries, own, held)
                result[u] = value.reshape(heads, BLK, head_dim)

            least = size
        copy(u).start()
        return carry

    lax.fori_loop(0, units, unit_body, 0)
    lax.fori_loop(0, units, lambda u, c: (copy(u).wait(), c)[1], 0)


def attend(place, table, queries, step_kv, parts, blocks_dev):
    steps, heads, tokens, head_dim = queries.shape
    units = steps * blocks_dev
    smem = pl.BlockSpec(memory_space=pltpu.SMEM)
    vmem = pl.BlockSpec(memory_space=pltpu.VMEM)
    return pl.pallas_call(
        functools.partial(attend_kernel, blocks_dev, len(parts)),
        in_specs=[smem, smem, vmem, vmem] + [vmem] * len(parts),
        out_specs=pl.BlockSpec(memory_space=pl.ANY),
        out_shape=jax.ShapeDtypeStruct(queries.shape, jnp.bfloat16),
        scratch_shapes=[
            pltpu.VMEM((2 * SLOTS * PAIR, 2 * head_dim), jnp.bfloat16),
            pltpu.VMEM((units, heads, BLK, head_dim), jnp.bfloat16),
            pltpu.SemaphoreType.DMA((units,)),
        ],
        compiler_params=pltpu.CompilerParams(vmem_limit_bytes=30 << 20),
        name="attend",
    )(place, table, queries, step_kv, *parts)


def per_device(features, norm_gain, kv_weight, queries, step_kv, doc_ids, block_lists):
    sections = lax.axis_size("section")
    seqs = lax.axis_size("seq")
    levels = seqs // 4
    step_total, local_heads, tok_dev, head_dim = queries.shape
    blocks_dev = tok_dev // BLK
    units = step_total * blocks_dev
    place = lax.axis_index("seq").reshape(1).astype(jnp.int32)

    partial = project(features, norm_gain, kv_weight, sections)
    parts = lax.all_to_all(partial, "section", 0, 0, tiled=True)
    kv = pl.pallas_call(
        functools.partial(reduce_kernel, float(features.shape[1] * sections)),
        out_shape=jax.ShapeDtypeStruct((tok_dev, 2 * head_dim), jnp.bfloat16),
        name="reduce",
    )(parts)

    lists = lax.dynamic_slice_in_dim(block_lists, place[0] * blocks_dev, blocks_dev, 1).reshape(units, LIST)
    table = pl.pallas_call(
        functools.partial(prepare_kernel, blocks_dev),
        in_specs=[pl.BlockSpec(memory_space=pltpu.SMEM)] * 2 + [pl.BlockSpec(memory_space=pltpu.VMEM)],
        out_specs=pl.BlockSpec(memory_space=pltpu.SMEM),
        out_shape=jax.ShapeDtypeStruct(((units + 1) * LINE,), jnp.int32),
        scratch_shapes=[pltpu.SMEM((block_lists.shape[1],), jnp.int32)],
        name="prepare",
    )(place, lists, doc_ids.reshape(-1, 128))

    every = range(seqs)
    swap = [(i, i ^ 1) for i in every]
    pair = jnp.concatenate([kv, lax.ppermute(kv, "seq", [(i, i ^ 2) for i in every])], axis=0)
    pair_theirs = lax.ppermute(pair, "seq", swap)
    up = down = pair
    ups, downs = [], []
    for d in range(1, 5):
        pairs = [(i, i + 4) for i in every if i // 4 + 1 < levels and i // 4 - d + 1 >= 0]
        up = lax.ppermute(up, "seq", pairs)
        ups.append(up)
        if d < 4:
            pairs = []
            for i in every:
                origin, goal = (i // 4 + d - 1) % levels, (i // 4 - 1) % levels
                if origin <= 2 and (goal < origin or goal >= 5):
                    pairs.append((i, (i - 4) % seqs))
            down = lax.ppermute(down, "seq", pairs)
            if d == 1:
                up, down, table, pair_theirs = lax.optimization_barrier((up, down, table, pair_theirs))
                ups[0] = up
            downs.append(down)
    near = jnp.concatenate([ups[0], ups[1], downs[1]], axis=0)
    far = jnp.concatenate([ups[2], downs[2]], axis=0)
    mine = [pair, near, far, ups[3]]
    theirs = [pair_theirs] + [lax.ppermute(a, "seq", swap) for a in mine[1:]]
    attended = attend(place, table, queries, step_kv, mine + theirs, blocks_dev)
    return attended, kv[None]


def solution(mesh):
    in_specs = (
        P("seq", "section"),
        P("section"),
        P("section", None),
        P(None, "section", "seq", None),
        P(None, "section", "seq", None),
        P(),
        P(),
    )
    out_specs = (P(None, "section", "seq", None), P("section", "seq", None))
    return jax.shard_map(per_device, mesh=mesh, in_specs=in_specs, out_specs=out_specs, check_vma=False)
```

```python
import functools
import math

import jax
import jax.numpy as jnp
from jax import lax
from jax.experimental import pallas as pl
from jax.experimental.pallas import tpu as pltpu
from jax.sharding import PartitionSpec as P

HEAD = 128
BLK = 64
LIST = 16
DOCS = 8
HIDDEN = -1e30
FAR = 1 << 24
EXTRA = 8
CHUNK = 128
NEAR_ROWS = 512
FAR_ROWS = 1280
LINE = 128
COUNTS = 64
NEAR_SIZES = (4, 8, 16)
FAR_SIZES = (0, 4, 8, 12, 16)

VMEM_ALL = 60 << 20


def project_kernel(feat, gain, weight, out, scaled, tail):
    tokens = feat.shape[0]

    @pl.when(pl.program_id(0) == 0)
    def _():
        x = feat[...].astype(jnp.float32)
        g = x * gain[...]
        high = g.astype(jnp.bfloat16)
        scaled[:tokens] = high
        scaled[tokens:] = (g - high.astype(jnp.float32)).astype(jnp.bfloat16)
        total = jnp.sum(x * x, axis=1, keepdims=True)
        row = jnp.broadcast_to(total, (tokens, 128)).T[:EXTRA]
        top = row.astype(jnp.bfloat16).astype(jnp.float32)
        which = lax.broadcasted_iota(jnp.int32, (EXTRA, 128), 0)
        tail[...] = jnp.where(which == 0, top, jnp.where(which == 1, row - top, 0.0)).astype(jnp.bfloat16)

    product = jnp.dot(scaled[...], weight[...], preferred_element_type=jnp.float32)
    product = (product[:tokens] + product[tokens:]).astype(jnp.bfloat16)
    cols = out.shape[2]
    for j in range(out.shape[0]):
        out[j, :tokens, :] = product[:, j * cols : (j + 1) * cols]
        out[j, tokens:, :128] = tail[...]
        out[j, tokens:, 128:] = jnp.zeros_like(tail)


def project(features, norm_gain, kv_weight, heads):
    tokens, width = features.shape
    cols = kv_weight.shape[1] // heads
    grid = 2
    return pl.pallas_call(
        project_kernel,
        grid=(grid,),
        in_specs=[
            pl.BlockSpec((tokens, width), lambda i: (0, 0)),
            pl.BlockSpec((1, width), lambda i: (0, 0)),
            pl.BlockSpec((width, kv_weight.shape[1] // grid), lambda i: (0, i)),
        ],
        out_specs=pl.BlockSpec((heads // grid, tokens + EXTRA, cols), lambda i: (i, 0, 0)),
        out_shape=jax.ShapeDtypeStruct((heads, tokens + EXTRA, cols), jnp.bfloat16),
        scratch_shapes=[
            pltpu.VMEM((2 * tokens, width), jnp.bfloat16),
            pltpu.VMEM((EXTRA, 128), jnp.bfloat16),
        ],
        compiler_params=pltpu.CompilerParams(vmem_limit_bytes=VMEM_ALL),
        name="project",
    )(features, norm_gain.reshape(1, width), kv_weight)


def reduce_kernel(width, parts, out, work):
    tokens = out.shape[0]
    total = jnp.sum(parts[:, tokens:, :128].astype(jnp.float32), axis=0)
    squares = jnp.broadcast_to(total[0:1] + total[1:2], (128, tokens)).T
    inverse = lax.rsqrt(squares / width + 1e-05)
    for half in range(2):
        cols = slice(half * 128, half * 128 + 128)
        kept = parts[0, :tokens, cols].astype(jnp.float32)
        for s in range(1, parts.shape[0]):
            kept = kept + parts[s, :tokens, cols].astype(jnp.float32)
        kept = (kept * inverse).astype(jnp.bfloat16)
        out[:, cols] = kept
        work[:, cols] = kept


def prepare_kernel(blocks_dev, place, lists, docs, table, seen):
    t = place[0]
    z = t // 4
    low = lax.rem(t, 4)
    units = lists.shape[0]
    d = docs[...]
    starts = [0] + [jnp.sum((d < doc).astype(jnp.int32)) for doc in range(1, DOCS)]
    for doc in range(DOCS):
        table[units * LINE + doc] = starts[doc]
    for c in range(seen.shape[0]):
        seen[c] = -1

    def unit_lists(u, carry):
        block = t * blocks_dev + lax.rem(u, blocks_dev)
        first = block * BLK
        begin = 0
        for doc in range(1, DOCS):
            begin = jnp.where(starts[doc] <= first, starts[doc], begin)
        least = begin // BLK
        base = u * LINE
        for e in range(LIST):
            table[base + e] = 0
            table[base + LIST + e] = FAR
            table[base + 2 * LIST + e] = 0
            table[base + 3 * LIST + e] = FAR
        near = 0
        far = 0
        for e in range(LIST):
            c = lists[u, e]
            keep = (c >= least) & (seen[c] != u)
            seen[c] = u
            away = z - c // 8
            x = lax.rem(c // 2, 4) ^ low
            inner = lax.rem(c, 2) * BLK
            y = x >> 1
            core = x & 1
            is_near = away <= 1
            near_row = core * NEAR_ROWS + away * (2 * CHUNK) + y * CHUNK + inner
            slot = jnp.where(away <= 3, away - 2, 8 - away)
            far_row = core * FAR_ROWS + y * (FAR_ROWS // 2) + slot * CHUNK + inner
            at = base + jnp.where(is_near, near, 2 * LIST + far)
            row = jnp.where(is_near, near_row, far_row)
            table[at] = jnp.where(keep, row, 0)
            table[at + LIST] = jnp.where(keep, c * BLK, FAR)
            near = near + (keep & is_near).astype(jnp.int32)
            far = far + (keep & ~is_near).astype(jnp.int32)
        counts = units * LINE + COUNTS + u
        table[counts] = near
        table[counts + units] = far
        return carry

    lax.fori_loop(0, units, unit_lists, 0)


def scores(blocks, base, block, extra, begins, table, queries, held):
    pieces = [held[pl.ds(pl.multiple_of(table[base + e], BLK), BLK), :] for e in range(blocks)]
    pieces += [rows for rows, _ in extra]
    kv = jnp.concatenate(pieces, axis=0)
    lane = lax.rem(lax.broadcasted_iota(jnp.int32, (1, 128), 1), BLK)
    sub = lax.broadcasted_iota(jnp.int32, (BLK, 128), 0)
    pos_i = block * BLK + lane
    masks = []
    for e in range(blocks):
        pos_j = table[base + LIST + e] + sub
        masks.append((pos_j >= begins) & (pos_j <= pos_i))
    masks += [(sub == lane) & allowed for _, allowed in extra]
    mask = jnp.concatenate(masks, axis=0)
    mask = jnp.concatenate([mask] * (queries.shape[0] // 128), axis=1)
    s = lax.dot_general(kv[:, :HEAD], queries, (((1,), (1,)), ((), ())), preferred_element_type=jnp.float32)
    return jnp.where(mask, s, HIDDEN), kv[:, HEAD:]


def weigh(p, values):
    return lax.dot_general(
        values, p.astype(jnp.bfloat16), (((0,), (0,)), ((), ())), preferred_element_type=jnp.float32
    )


def unit_state(blocks_dev, u, t, table, q):
    steps, heads, tokens, head_dim = q.shape
    units = steps * blocks_dev
    k = u // blocks_dev
    half = lax.rem(u, blocks_dev)
    block = t * blocks_dev + half
    rows = pl.ds(pl.multiple_of(half * BLK, BLK), BLK)
    queries = q[k, :, rows, :].reshape(heads * BLK, head_dim)
    pos_i = block * BLK + lax.rem(lax.broadcasted_iota(jnp.int32, (1, 128), 1), BLK)
    begins = jnp.zeros((1, 128), jnp.int32)
    for doc in range(1, DOCS):
        start = table[units * LINE + doc]
        begins = jnp.where(start <= pos_i, start, begins)
    return k, block, rows, queries, begins


def per_size(sizes, n, run):
    least = -1
    for size in sizes:
        pl.when((n > least) & (n <= size))(functools.partial(run, size))
        least = size


SCALE = math.log2(math.e) / math.sqrt(HEAD)


def near_kernel(blocks_dev, place, table, q, own, mine, theirs, state, sums, held):
    t = place[0]
    units = q.shape[0] * blocks_dev
    held[:NEAR_ROWS] = mine[...]
    held[NEAR_ROWS:] = theirs[...]

    def body(u, carry):
        k, block, rows, queries, begins = unit_state(blocks_dev, u, t, table, q)

        def run(size):
            extra = [(own[m, 0, rows, :], m <= k) for m in range(own.shape[0])]
            s, values = scores(size, u * LINE, block, extra, begins, table, queries, held)
            top = jnp.max(s, axis=0, keepdims=True)
            p = jnp.exp2((s - top) * SCALE)
            sums[u, 0:1] = top
            sums[u, 1:2] = jnp.sum(p, axis=0, keepdims=True)
            state[u] = weigh(p, values)

        per_size(NEAR_SIZES, table[units * LINE + COUNTS + u], run)
        return carry

    lax.fori_loop(0, units, body, 0)


def far_kernel(blocks_dev, place, table, q, state, sums, mine, theirs, out, held, result, sems):
    t = place[0]
    steps, heads, tokens, head_dim = q.shape
    units = steps * blocks_dev
    held[:FAR_ROWS] = mine[...]
    held[FAR_ROWS:] = theirs[...]

    def copy(u):
        rows = pl.ds(pl.multiple_of(lax.rem(u, blocks_dev) * BLK, BLK), BLK)
        return pltpu.make_async_copy(result.at[u], out.at[u // blocks_dev, :, rows, :], sems.at[u])

    def body(u, carry):
        k, block, rows, queries, begins = unit_state(blocks_dev, u, t, table, q)

        def run(size):
            top, total, summed = sums[u, 0:1], sums[u, 1:2], state[u]
            if size:
                s, values = scores(size, u * LINE + 2 * LIST, block, [], begins, table, queries, held)
                new_top = jnp.maximum(top, jnp.max(s, axis=0, keepdims=True))
                p = jnp.exp2((s - new_top) * SCALE)
                factor = jnp.exp2((top - new_top) * SCALE)
                total = total * factor + jnp.sum(p, axis=0, keepdims=True)
                summed = summed * factor + weigh(p, values)
            result[u] = (summed / total).T.astype(jnp.bfloat16).reshape(heads, BLK, head_dim)

        per_size(FAR_SIZES, table[units * LINE + COUNTS + units + u], run)
        copy(u).start()
        return carry

    lax.fori_loop(0, units, body, 0)
    lax.fori_loop(0, units, lambda u, c: (copy(u).wait(), c)[1], 0)


SMEM_ALL = pl.BlockSpec(memory_space=pltpu.SMEM)
VMEM_WHOLE = pl.BlockSpec(memory_space=pltpu.VMEM)


def limit(mib):
    return pltpu.CompilerParams(vmem_limit_bytes=mib << 20)


def attend_near(place, table, queries, step_kv, mine, theirs, blocks_dev):
    steps, heads, tokens, head_dim = queries.shape
    units = steps * blocks_dev
    return pl.pallas_call(
        functools.partial(near_kernel, blocks_dev),
        in_specs=[SMEM_ALL, SMEM_ALL] + [VMEM_WHOLE] * 4,
        out_specs=[VMEM_WHOLE, VMEM_WHOLE],
        out_shape=[
            jax.ShapeDtypeStruct((units, head_dim, heads * BLK), jnp.float32),
            jax.ShapeDtypeStruct((units, 8, heads * BLK), jnp.float32),
        ],
        scratch_shapes=[pltpu.VMEM((2 * NEAR_ROWS, 2 * head_dim), jnp.bfloat16)],
        compiler_params=limit(24),
        name="attend_near",
    )(place, table, queries, step_kv, mine, theirs)


def attend_far(place, table, queries, state, sums, mine, theirs, blocks_dev):
    steps, heads, tokens, head_dim = queries.shape
    units = steps * blocks_dev
    return pl.pallas_call(
        functools.partial(far_kernel, blocks_dev),
        in_specs=[SMEM_ALL, SMEM_ALL] + [VMEM_WHOLE] * 5,
        out_specs=pl.BlockSpec(memory_space=pl.ANY),
        out_shape=jax.ShapeDtypeStruct(queries.shape, jnp.bfloat16),
        scratch_shapes=[
            pltpu.VMEM((2 * FAR_ROWS, 2 * head_dim), jnp.bfloat16),
            pltpu.VMEM((units, heads, BLK, head_dim), jnp.bfloat16),
            pltpu.SemaphoreType.DMA((units,)),
        ],
        compiler_params=limit(24),
        name="attend_far",
    )(place, table, queries, state, sums, mine, theirs)


def per_device(features, norm_gain, kv_weight, queries, step_kv, doc_ids, block_lists):
    sections = lax.axis_size("section")
    seqs = lax.axis_size("seq")
    step_total, local_heads, tok_dev, head_dim = queries.shape
    blocks_dev = tok_dev // BLK
    units = step_total * blocks_dev
    place = lax.axis_index("seq").reshape(1).astype(jnp.int32)

    partial = project(features, norm_gain, kv_weight, sections)
    parts = lax.all_to_all(partial, "section", 0, 0, tiled=True)
    kv_cache, kv = pl.pallas_call(
        functools.partial(reduce_kernel, float(features.shape[1] * sections)),
        out_shape=[jax.ShapeDtypeStruct((tok_dev, 2 * head_dim), jnp.bfloat16)] * 2,
        compiler_params=limit(8),
        name="reduce",
    )(parts)

    lists = lax.dynamic_slice_in_dim(block_lists, place[0] * blocks_dev, blocks_dev, 1).reshape(units, LIST)
    table = pl.pallas_call(
        functools.partial(prepare_kernel, blocks_dev),
        in_specs=[SMEM_ALL, SMEM_ALL, VMEM_WHOLE],
        out_specs=SMEM_ALL,
        out_shape=jax.ShapeDtypeStruct(((units + 1) * LINE,), jnp.int32),
        scratch_shapes=[pltpu.SMEM((block_lists.shape[1],), jnp.int32)],
        compiler_params=limit(4),
        name="prepare",
    )(place, lists, doc_ids.reshape(-1, 128))

    every = range(seqs)

    def along_z(x, levels):
        return lax.ppermute(x, "seq", [(i, (i + 4 * levels) % seqs) for i in every])

    def along_y(x):
        return lax.ppermute(x, "seq", [(i, i ^ 2) for i in every])

    def along_core(x):
        return lax.ppermute(x, "seq", [(i, i ^ 1) for i in every])

    def join(*arrays):
        return jnp.concatenate(arrays, axis=0)

    own_y = along_y(kv)
    up1 = along_z(kv, 1)
    down1 = along_z(kv, -1)
    up4 = along_z(kv, 4)
    up23 = along_z(join(kv, up1), 2)
    down23 = along_z(join(kv, down1), -2)
    near = join(kv, own_y, up1, along_y(up1))
    near_other = along_core(near)
    up23, down23, table = lax.optimization_barrier((up23, down23, table))
    far = join(up23, down23, up4)
    far_y = along_y(far)
    state, sums = attend_near(place, table, queries, step_kv, near, near_other, blocks_dev)
    far_y, state, sums = lax.optimization_barrier((far_y, state, sums))
    far = join(far, far_y)
    attended = attend_far(place, table, queries, state, sums, far, along_core(far), blocks_dev)
    return attended, kv_cache[None]


def solution(mesh):
    in_specs = (
        P("seq", "section"),
        P("section"),
        P("section", None),
        P(None, "section", "seq", None),
        P(None, "section", "seq", None),
        P(),
        P(),
    )
    out_specs = (P(None, "section", "seq", None), P("section", "seq", None))
    return jax.shard_map(per_device, mesh=mesh, in_specs=in_specs, out_specs=out_specs, check_vma=False)
```

```python
import functools
import math

import jax
import jax.numpy as jnp
from jax import lax
from jax.experimental import pallas as pl
from jax.experimental.pallas import tpu as pltpu
from jax.sharding import PartitionSpec as P

HEAD = 128
BLK = 64
LIST = 16
DOCS = 8
HIDDEN = -1e30
FAR = 1 << 24
EXTRA = 8
CHUNK = 128
NEAR_ROWS = 512
FAR_ROWS = 640
LINE = 128
COUNTS = 64
NEAR_SIZES = (4, 8, 12, 16)
FAR_SIZES = (0, 2, 4, 6, 8, 16)

VMEM_ALL = 60 << 20


def project_kernel(feat, gain, weight, out, scaled, tail):
    tokens = feat.shape[0]

    @pl.when(pl.program_id(0) == 0)
    def _():
        x = feat[...].astype(jnp.float32)
        g = x * gain[...]
        high = g.astype(jnp.bfloat16)
        scaled[:tokens] = high
        scaled[tokens:] = (g - high.astype(jnp.float32)).astype(jnp.bfloat16)
        total = jnp.sum(x * x, axis=1, keepdims=True)
        row = jnp.broadcast_to(total, (tokens, 128)).T[:EXTRA]
        top = row.astype(jnp.bfloat16).astype(jnp.float32)
        which = lax.broadcasted_iota(jnp.int32, (EXTRA, 128), 0)
        tail[...] = jnp.where(which == 0, top, jnp.where(which == 1, row - top, 0.0)).astype(jnp.bfloat16)

    product = jnp.dot(scaled[...], weight[...], preferred_element_type=jnp.float32)
    product = (product[:tokens] + product[tokens:]).astype(jnp.bfloat16)
    cols = out.shape[2]
    for j in range(out.shape[0]):
        out[j, :tokens, :] = product[:, j * cols : (j + 1) * cols]
        out[j, tokens:, :128] = tail[...]
        out[j, tokens:, 128:] = jnp.zeros_like(tail)


def project(features, norm_gain, kv_weight, heads):
    tokens, width = features.shape
    cols = kv_weight.shape[1] // heads
    grid = 2
    return pl.pallas_call(
        project_kernel,
        grid=(grid,),
        in_specs=[
            pl.BlockSpec((tokens, width), lambda i: (0, 0)),
            pl.BlockSpec((1, width), lambda i: (0, 0)),
            pl.BlockSpec((width, kv_weight.shape[1] // grid), lambda i: (0, i)),
        ],
        out_specs=pl.BlockSpec((heads // grid, tokens + EXTRA, cols), lambda i: (i, 0, 0)),
        out_shape=jax.ShapeDtypeStruct((heads, tokens + EXTRA, cols), jnp.bfloat16),
        scratch_shapes=[
            pltpu.VMEM((2 * tokens, width), jnp.bfloat16),
            pltpu.VMEM((EXTRA, 128), jnp.bfloat16),
        ],
        compiler_params=pltpu.CompilerParams(vmem_limit_bytes=VMEM_ALL),
        name="project",
    )(features, norm_gain.reshape(1, width), kv_weight)


def reduce_kernel(width, parts, out, work):
    tokens = out.shape[0]
    total = jnp.sum(parts[:, tokens:, :128].astype(jnp.float32), axis=0)
    squares = jnp.broadcast_to(total[0:1] + total[1:2], (128, tokens)).T
    inverse = lax.rsqrt(squares / width + 1e-05)
    for half in range(2):
        cols = slice(half * 128, half * 128 + 128)
        kept = parts[0, :tokens, cols].astype(jnp.float32)
        for s in range(1, parts.shape[0]):
            kept = kept + parts[s, :tokens, cols].astype(jnp.float32)
        kept = (kept * inverse).astype(jnp.bfloat16)
        out[:, cols] = kept
        work[:, cols] = kept


def prepare_kernel(blocks_dev, place, lists, docs, table, seen):
    t = place[0]
    z = t // 4
    low = lax.rem(t, 4)
    units = lists.shape[0]
    d = docs[...]
    starts = [0] + [jnp.sum((d < doc).astype(jnp.int32)) for doc in range(1, DOCS)]
    for doc in range(DOCS):
        table[units * LINE + doc] = starts[doc]
    for c in range(seen.shape[0]):
        seen[c] = -1

    def unit_lists(u, carry):
        block = t * blocks_dev + lax.rem(u, blocks_dev)
        first = block * BLK
        begin = 0
        for doc in range(1, DOCS):
            begin = jnp.where(starts[doc] <= first, starts[doc], begin)
        least = begin // BLK
        base = u * LINE
        for e in range(LIST):
            table[base + e] = 0
            table[base + LIST + e] = FAR
            table[base + 2 * LIST + e] = 0
            table[base + 3 * LIST + e] = FAR
        near = 0
        far = 0
        for e in range(LIST):
            c = lists[u, e]
            keep = (c >= least) & (seen[c] != u)
            seen[c] = u
            away = z - c // 8
            x = lax.rem(c // 2, 4) ^ low
            inner = lax.rem(c, 2) * BLK
            y = x >> 1
            core = x & 1
            is_near = (away <= 1) | (y == 0)
            slot = jnp.where(away <= 3, away - 2, 8 - away)
            far_row = core * FAR_ROWS + slot * CHUNK + inner
            near_row = core * (NEAR_ROWS + FAR_ROWS) + inner
            near_row += jnp.where(away <= 1, away * (2 * CHUNK) + y * CHUNK, NEAR_ROWS + slot * CHUNK)
            at = base + jnp.where(is_near, near, 2 * LIST + far)
            row = jnp.where(is_near, near_row, far_row)
            table[at] = jnp.where(keep, row, 0)
            table[at + LIST] = jnp.where(keep, c * BLK, FAR)
            near = near + (keep & is_near).astype(jnp.int32)
            far = far + (keep & ~is_near).astype(jnp.int32)
        counts = units * LINE + COUNTS + u
        table[counts] = near
        table[counts + units] = far
        return carry

    lax.fori_loop(0, units, unit_lists, 0)


def scores(blocks, base, block, extra, begins, table, queries, held):
    pieces = [held[pl.ds(pl.multiple_of(table[base + e], BLK), BLK), :] for e in range(blocks)]
    pieces += [rows for rows, _ in extra]
    kv = jnp.concatenate(pieces, axis=0)
    lane = lax.rem(lax.broadcasted_iota(jnp.int32, (1, 128), 1), BLK)
    sub = lax.broadcasted_iota(jnp.int32, (BLK, 128), 0)
    pos_i = block * BLK + lane
    masks = []
    for e in range(blocks):
        pos_j = table[base + LIST + e] + sub
        masks.append((pos_j >= begins) & (pos_j <= pos_i))
    masks += [(sub == lane) & allowed for _, allowed in extra]
    mask = jnp.concatenate(masks, axis=0)
    mask = jnp.concatenate([mask] * (queries.shape[0] // 128), axis=1)
    s = lax.dot_general(kv[:, :HEAD], queries, (((1,), (1,)), ((), ())), preferred_element_type=jnp.float32)
    return jnp.where(mask, s, HIDDEN), kv[:, HEAD:]


def weigh(p, values):
    return lax.dot_general(
        values, p.astype(jnp.bfloat16), (((0,), (0,)), ((), ())), preferred_element_type=jnp.float32
    )


def unit_state(blocks_dev, u, t, table, q):
    steps, heads, tokens, head_dim = q.shape
    units = steps * blocks_dev
    k = u // blocks_dev
    half = lax.rem(u, blocks_dev)
    block = t * blocks_dev + half
    rows = pl.ds(pl.multiple_of(half * BLK, BLK), BLK)
    queries = q[k, :, rows, :].reshape(heads * BLK, head_dim)
    pos_i = block * BLK + lax.rem(lax.broadcasted_iota(jnp.int32, (1, 128), 1), BLK)
    begins = jnp.zeros((1, 128), jnp.int32)
    for doc in range(1, DOCS):
        start = table[units * LINE + doc]
        begins = jnp.where(start <= pos_i, start, begins)
    return k, block, rows, queries, begins


def per_size(sizes, n, run):
    least = -1
    for size in sizes:
        pl.when((n > least) & (n <= size))(functools.partial(run, size))
        least = size


SCALE = math.log2(math.e) / math.sqrt(HEAD)


def hold(held, parts):
    row = 0
    for part in parts:
        held[row : row + part.shape[0]] = part[...]
        row += part.shape[0]


def near_kernel(blocks_dev, place, table, q, own, mine, theirs, state, sums, held):
    t = place[0]
    units = q.shape[0] * blocks_dev
    hold(held, (mine, theirs))

    def body(u, carry):
        k, block, rows, queries, begins = unit_state(blocks_dev, u, t, table, q)

        def run(size):
            extra = [(own[m, 0, rows, :], m <= k) for m in range(own.shape[0])]
            s, values = scores(size, u * LINE, block, extra, begins, table, queries, held)
            top = jnp.max(s, axis=0, keepdims=True)
            p = jnp.exp2((s - top) * SCALE)
            sums[u, 0:1] = top
            sums[u, 1:2] = jnp.sum(p, axis=0, keepdims=True)
            state[u] = weigh(p, values)

        per_size(NEAR_SIZES, table[units * LINE + COUNTS + u], run)
        return carry

    lax.fori_loop(0, units, body, 0)


def far_kernel(blocks_dev, place, table, q, state, sums, mine, theirs, out, held, result, sems):
    t = place[0]
    steps, heads, tokens, head_dim = q.shape
    units = steps * blocks_dev
    hold(held, (mine, theirs))

    def copy(u):
        rows = pl.ds(pl.multiple_of(lax.rem(u, blocks_dev) * BLK, BLK), BLK)
        return pltpu.make_async_copy(result.at[u], out.at[u // blocks_dev, :, rows, :], sems.at[u])

    def body(u, carry):
        k, block, rows, queries, begins = unit_state(blocks_dev, u, t, table, q)

        def run(size):
            top, total, summed = sums[u, 0:1], sums[u, 1:2], state[u]
            if size:
                s, values = scores(size, u * LINE + 2 * LIST, block, [], begins, table, queries, held)
                new_top = jnp.maximum(top, jnp.max(s, axis=0, keepdims=True))
                p = jnp.exp2((s - new_top) * SCALE)
                factor = jnp.exp2((top - new_top) * SCALE)
                total = total * factor + jnp.sum(p, axis=0, keepdims=True)
                summed = summed * factor + weigh(p, values)
            result[u] = (summed / total).T.astype(jnp.bfloat16).reshape(heads, BLK, head_dim)

        per_size(FAR_SIZES, table[units * LINE + COUNTS + units + u], run)
        copy(u).start()
        return carry

    lax.fori_loop(0, units, body, 0)
    lax.fori_loop(0, units, lambda u, c: (copy(u).wait(), c)[1], 0)


SMEM_ALL = pl.BlockSpec(memory_space=pltpu.SMEM)
VMEM_WHOLE = pl.BlockSpec(memory_space=pltpu.VMEM)


def limit(mib):
    return pltpu.CompilerParams(vmem_limit_bytes=mib << 20)


def attend_near(place, table, queries, step_kv, parts, blocks_dev):
    steps, heads, tokens, head_dim = queries.shape
    units = steps * blocks_dev
    return pl.pallas_call(
        functools.partial(near_kernel, blocks_dev),
        in_specs=[SMEM_ALL, SMEM_ALL] + [VMEM_WHOLE] * (2 + len(parts)),
        out_specs=[VMEM_WHOLE, VMEM_WHOLE],
        out_shape=[
            jax.ShapeDtypeStruct((units, head_dim, heads * BLK), jnp.float32),
            jax.ShapeDtypeStruct((units, 8, heads * BLK), jnp.float32),
        ],
        scratch_shapes=[pltpu.VMEM((2 * (NEAR_ROWS + FAR_ROWS), 2 * head_dim), jnp.bfloat16)],
        compiler_params=limit(24),
        name="attend_near",
    )(place, table, queries, step_kv, *parts)


def attend_far(place, table, queries, state, sums, mine, theirs, blocks_dev):
    steps, heads, tokens, head_dim = queries.shape
    units = steps * blocks_dev
    return pl.pallas_call(
        functools.partial(far_kernel, blocks_dev),
        in_specs=[SMEM_ALL, SMEM_ALL] + [VMEM_WHOLE] * 5,
        out_specs=pl.BlockSpec(memory_space=pl.ANY),
        out_shape=jax.ShapeDtypeStruct(queries.shape, jnp.bfloat16),
        scratch_shapes=[
            pltpu.VMEM((2 * FAR_ROWS, 2 * head_dim), jnp.bfloat16),
            pltpu.VMEM((units, heads, BLK, head_dim), jnp.bfloat16),
            pltpu.SemaphoreType.DMA((units,)),
        ],
        compiler_params=limit(24),
        name="attend_far",
    )(place, table, queries, state, sums, mine, theirs)


def per_device(features, norm_gain, kv_weight, queries, step_kv, doc_ids, block_lists):
    sections = lax.axis_size("section")
    seqs = lax.axis_size("seq")
    step_total, local_heads, tok_dev, head_dim = queries.shape
    blocks_dev = tok_dev // BLK
    units = step_total * blocks_dev
    place = lax.axis_index("seq").reshape(1).astype(jnp.int32)

    partial = project(features, norm_gain, kv_weight, sections)
    parts = lax.all_to_all(partial, "section", 0, 0, tiled=True)
    lists = lax.dynamic_slice_in_dim(block_lists, place[0] * blocks_dev, blocks_dev, 1).reshape(units, LIST)
    table = pl.pallas_call(
        functools.partial(prepare_kernel, blocks_dev),
        in_specs=[SMEM_ALL, SMEM_ALL, VMEM_WHOLE],
        out_specs=SMEM_ALL,
        out_shape=jax.ShapeDtypeStruct(((units + 1) * LINE,), jnp.int32),
        scratch_shapes=[pltpu.SMEM((block_lists.shape[1],), jnp.int32)],
        compiler_params=limit(4),
        name="prepare",
    )(place, lists, doc_ids.reshape(-1, 128))

    parts, table = lax.optimization_barrier((parts, table))
    kv_cache, kv = pl.pallas_call(
        functools.partial(reduce_kernel, float(features.shape[1] * sections)),
        out_shape=[jax.ShapeDtypeStruct((tok_dev, 2 * head_dim), jnp.bfloat16)] * 2,
        compiler_params=limit(8),
        name="reduce",
    )(parts)

    every = range(seqs)

    def along_z(x, levels):
        return lax.ppermute(x, "seq", [(i, (i + 4 * levels) % seqs) for i in every])

    def along_y(x):
        return lax.ppermute(x, "seq", [(i, i ^ 2) for i in every])

    def along_core(x):
        return lax.ppermute(x, "seq", [(i, i ^ 1) for i in every])

    def join(*arrays):
        return jnp.concatenate(arrays, axis=0)

    up1 = along_z(kv, 1)
    down1 = along_z(kv, -1)
    own_y = along_y(kv)
    low, high = join(kv, up1), join(kv, down1)
    low, high = lax.optimization_barrier((low, high))
    up23 = along_z(low, 2)
    down23 = along_z(high, -2)
    kept, _, _, _ = lax.optimization_barrier((kv, low, high, own_y))
    up4 = along_z(kept, 4)
    up1_y = along_y(up1)
    column = join(up23, down23, up4)
    far = along_y(column)
    near = join(kv, own_y, up1, up1_y, column)
    state, sums = attend_near(place, table, queries, step_kv, (near, along_core(near)), blocks_dev)
    far, state, sums = lax.optimization_barrier((far, state, sums))
    attended = attend_far(place, table, queries, state, sums, far, along_core(far), blocks_dev)
    return attended, kv_cache[None]


def solution(mesh):
    in_specs = (
        P("seq", "section"),
        P("section"),
        P("section", None),
        P(None, "section", "seq", None),
        P(None, "section", "seq", None),
        P(),
        P(),
    )
    out_specs = (P(None, "section", "seq", None), P("section", "seq", None))
    return jax.shard_map(per_device, mesh=mesh, in_specs=in_specs, out_specs=out_specs, check_vma=False)
```

```python
import functools
import math

import jax
import jax.numpy as jnp
from jax import lax
from jax.experimental import pallas as pl
from jax.experimental.pallas import tpu as pltpu
from jax.sharding import PartitionSpec as P

HEAD = 128
BLK = 64
LIST = 16
DOCS = 8
HIDDEN = -1e30
FAR = 1 << 24
EXTRA = 8
CHUNK = 128
NEAR_ROWS = 512
FAR_ROWS = 640
LINE = 128
COUNTS = 64
NEAR_SIZES = (4, 8, 12, 16)
FAR_SIZES = (0, 2, 4, 6, 8, 16)

VMEM_ALL = 60 << 20


def project_kernel(feat, gain, weight, out, scaled, tail):
    tokens = feat.shape[0]

    @pl.when(pl.program_id(0) == 0)
    def _():
        x = feat[...].astype(jnp.float32)
        g = x * gain[...]
        high = g.astype(jnp.bfloat16)
        scaled[:tokens] = high
        scaled[tokens:] = (g - high.astype(jnp.float32)).astype(jnp.bfloat16)
        total = jnp.sum(x * x, axis=1, keepdims=True)
        row = jnp.broadcast_to(total, (tokens, 128)).T[:EXTRA]
        top = row.astype(jnp.bfloat16).astype(jnp.float32)
        which = lax.broadcasted_iota(jnp.int32, (EXTRA, 128), 0)
        tail[...] = jnp.where(which == 0, top, jnp.where(which == 1, row - top, 0.0)).astype(jnp.bfloat16)

    product = jnp.dot(scaled[...], weight[...], preferred_element_type=jnp.float32)
    product = (product[:tokens] + product[tokens:]).astype(jnp.bfloat16)
    cols = out.shape[2]
    for j in range(out.shape[0]):
        out[j, :tokens, :] = product[:, j * cols : (j + 1) * cols]
        out[j, tokens:, :128] = tail[...]
        out[j, tokens:, 128:] = jnp.zeros_like(tail)


def project(features, norm_gain, kv_weight, heads):
    tokens, width = features.shape
    cols = kv_weight.shape[1] // heads
    grid = 2
    return pl.pallas_call(
        project_kernel,
        grid=(grid,),
        in_specs=[
            pl.BlockSpec((tokens, width), lambda i: (0, 0)),
            pl.BlockSpec((1, width), lambda i: (0, 0)),
            pl.BlockSpec((width, kv_weight.shape[1] // grid), lambda i: (0, i)),
        ],
        out_specs=pl.BlockSpec((heads // grid, tokens + EXTRA, cols), lambda i: (i, 0, 0)),
        out_shape=jax.ShapeDtypeStruct((heads, tokens + EXTRA, cols), jnp.bfloat16),
        scratch_shapes=[
            pltpu.VMEM((2 * tokens, width), jnp.bfloat16),
            pltpu.VMEM((EXTRA, 128), jnp.bfloat16),
        ],
        compiler_params=pltpu.CompilerParams(vmem_limit_bytes=VMEM_ALL),
        name="project",
    )(features, norm_gain.reshape(1, width), kv_weight)


def reduce_kernel(width, parts, out, work):
    tokens = out.shape[0]
    total = jnp.sum(parts[:, tokens:, :128].astype(jnp.float32), axis=0)
    squares = jnp.broadcast_to(total[0:1] + total[1:2], (128, tokens)).T
    inverse = lax.rsqrt(squares / width + 1e-05)
    for half in range(2):
        cols = slice(half * 128, half * 128 + 128)
        kept = parts[0, :tokens, cols].astype(jnp.float32)
        for s in range(1, parts.shape[0]):
            kept = kept + parts[s, :tokens, cols].astype(jnp.float32)
        kept = (kept * inverse).astype(jnp.bfloat16)
        out[:, cols] = kept
        work[:, cols] = kept


def prepare_kernel(blocks_dev, place, lists, docs, table, seen):
    t = place[0]
    z = t // 4
    low = lax.rem(t, 4)
    units = lists.shape[0]
    d = docs[...]
    starts = [0] + [jnp.sum((d < doc).astype(jnp.int32)) for doc in range(1, DOCS)]
    for doc in range(DOCS):
        table[units * LINE + doc] = starts[doc]
    for c in range(seen.shape[0]):
        seen[c] = -1

    def unit_lists(u, carry):
        block = t * blocks_dev + lax.rem(u, blocks_dev)
        first = block * BLK
        begin = 0
        for doc in range(1, DOCS):
            begin = jnp.where(starts[doc] <= first, starts[doc], begin)
        least = begin // BLK
        base = u * LINE
        for e in range(LIST):
            table[base + e] = 0
            table[base + LIST + e] = FAR
            table[base + 2 * LIST + e] = 0
            table[base + 3 * LIST + e] = FAR
        near = 0
        far = 0
        for e in range(LIST):
            c = lists[u, e]
            keep = (c >= least) & (seen[c] != u)
            seen[c] = u
            away = z - c // 8
            x = lax.rem(c // 2, 4) ^ low
            inner = lax.rem(c, 2) * BLK
            y = x >> 1
            core = x & 1
            is_near = (away <= 1) | (y == 0)
            slot = jnp.where(away <= 3, away - 2, 8 - away)
            far_row = core * FAR_ROWS + slot * CHUNK + inner
            near_row = core * (NEAR_ROWS + FAR_ROWS) + inner
            near_row += jnp.where(away <= 1, y * (2 * CHUNK) + away * CHUNK, NEAR_ROWS + slot * CHUNK)
            at = base + jnp.where(is_near, near, 2 * LIST + far)
            row = jnp.where(is_near, near_row, far_row)
            table[at] = jnp.where(keep, row, 0)
            table[at + LIST] = jnp.where(keep, c * BLK, FAR)
            near = near + (keep & is_near).astype(jnp.int32)
            far = far + (keep & ~is_near).astype(jnp.int32)
        counts = units * LINE + COUNTS + u
        table[counts] = near
        table[counts + units] = far
        return carry

    lax.fori_loop(0, units, unit_lists, 0)


def scores(blocks, base, block, extra, begins, table, queries, held):
    pieces = [held[pl.ds(pl.multiple_of(table[base + e], BLK), BLK), :] for e in range(blocks)]
    pieces += [rows for rows, _ in extra]
    kv = jnp.concatenate(pieces, axis=0)
    lane = lax.rem(lax.broadcasted_iota(jnp.int32, (1, 128), 1), BLK)
    sub = lax.broadcasted_iota(jnp.int32, (BLK, 128), 0)
    pos_i = block * BLK + lane
    masks = []
    for e in range(blocks):
        pos_j = table[base + LIST + e] + sub
        masks.append((pos_j >= begins) & (pos_j <= pos_i))
    masks += [(sub == lane) & allowed for _, allowed in extra]
    mask = jnp.concatenate(masks, axis=0)
    mask = jnp.concatenate([mask] * (queries.shape[0] // 128), axis=1)
    s = lax.dot_general(kv[:, :HEAD], queries, (((1,), (1,)), ((), ())), preferred_element_type=jnp.float32)
    return jnp.where(mask, s, HIDDEN), kv[:, HEAD:]


def weigh(p, values):
    return lax.dot_general(
        values, p.astype(jnp.bfloat16), (((0,), (0,)), ((), ())), preferred_element_type=jnp.float32
    )


def unit_state(blocks_dev, u, t, table, q):
    steps, heads, tokens, head_dim = q.shape
    units = steps * blocks_dev
    k = u // blocks_dev
    half = lax.rem(u, blocks_dev)
    block = t * blocks_dev + half
    rows = pl.ds(pl.multiple_of(half * BLK, BLK), BLK)
    queries = q[k, :, rows, :].reshape(heads * BLK, head_dim)
    pos_i = block * BLK + lax.rem(lax.broadcasted_iota(jnp.int32, (1, 128), 1), BLK)
    begins = jnp.zeros((1, 128), jnp.int32)
    for doc in range(1, DOCS):
        start = table[units * LINE + doc]
        begins = jnp.where(start <= pos_i, start, begins)
    return k, block, rows, queries, begins


def per_size(sizes, n, run):
    least = -1
    for size in sizes:
        pl.when((n > least) & (n <= size))(functools.partial(run, size))
        least = size


SCALE = math.log2(math.e) / math.sqrt(HEAD)


def hold(held, parts):
    row = 0
    for part in parts:
        held[row : row + part.shape[0]] = part[...]
        row += part.shape[0]


def near_kernel(blocks_dev, place, table, q, own, mine, theirs, state, sums, held):
    t = place[0]
    units = q.shape[0] * blocks_dev
    hold(held, (mine, theirs))

    def body(u, carry):
        k, block, rows, queries, begins = unit_state(blocks_dev, u, t, table, q)

        def run(size):
            extra = [(own[m, 0, rows, :], m <= k) for m in range(own.shape[0])]
            s, values = scores(size, u * LINE, block, extra, begins, table, queries, held)
            top = jnp.max(s, axis=0, keepdims=True)
            p = jnp.exp2((s - top) * SCALE)
            sums[u, 0:1] = top
            sums[u, 1:2] = jnp.sum(p, axis=0, keepdims=True)
            state[u] = weigh(p, values)

        per_size(NEAR_SIZES, table[units * LINE + COUNTS + u], run)
        return carry

    lax.fori_loop(0, units, body, 0)


def far_kernel(blocks_dev, place, table, q, state, sums, mine, theirs, out, held, result, sems):
    t = place[0]
    steps, heads, tokens, head_dim = q.shape
    units = steps * blocks_dev
    hold(held, (mine, theirs))

    def copy(u):
        rows = pl.ds(pl.multiple_of(lax.rem(u, blocks_dev) * BLK, BLK), BLK)
        return pltpu.make_async_copy(result.at[u], out.at[u // blocks_dev, :, rows, :], sems.at[u])

    def body(u, carry):
        k, block, rows, queries, begins = unit_state(blocks_dev, u, t, table, q)

        def run(size):
            top, total, summed = sums[u, 0:1], sums[u, 1:2], state[u]
            if size:
                s, values = scores(size, u * LINE + 2 * LIST, block, [], begins, table, queries, held)
                new_top = jnp.maximum(top, jnp.max(s, axis=0, keepdims=True))
                p = jnp.exp2((s - new_top) * SCALE)
                factor = jnp.exp2((top - new_top) * SCALE)
                total = total * factor + jnp.sum(p, axis=0, keepdims=True)
                summed = summed * factor + weigh(p, values)
            result[u] = (summed * (1.0 / total)).T.astype(jnp.bfloat16).reshape(heads, BLK, head_dim)

        per_size(FAR_SIZES, table[units * LINE + COUNTS + units + u], run)
        copy(u).start()
        return carry

    lax.fori_loop(0, units, body, 0)
    lax.fori_loop(0, units, lambda u, c: (copy(u).wait(), c)[1], 0)


SMEM_ALL = pl.BlockSpec(memory_space=pltpu.SMEM)
VMEM_WHOLE = pl.BlockSpec(memory_space=pltpu.VMEM)


def limit(mib):
    return pltpu.CompilerParams(vmem_limit_bytes=mib << 20)


def attend_near(place, table, queries, step_kv, parts, blocks_dev):
    steps, heads, tokens, head_dim = queries.shape
    units = steps * blocks_dev
    return pl.pallas_call(
        functools.partial(near_kernel, blocks_dev),
        in_specs=[SMEM_ALL, SMEM_ALL] + [VMEM_WHOLE] * (2 + len(parts)),
        out_specs=[VMEM_WHOLE, VMEM_WHOLE],
        out_shape=[
            jax.ShapeDtypeStruct((units, head_dim, heads * BLK), jnp.float32),
            jax.ShapeDtypeStruct((units, 8, heads * BLK), jnp.float32),
        ],
        scratch_shapes=[pltpu.VMEM((2 * (NEAR_ROWS + FAR_ROWS), 2 * head_dim), jnp.bfloat16)],
        compiler_params=limit(24),
        name="attend_near",
    )(place, table, queries, step_kv, *parts)


def attend_far(place, table, queries, state, sums, mine, theirs, blocks_dev):
    steps, heads, tokens, head_dim = queries.shape
    units = steps * blocks_dev
    return pl.pallas_call(
        functools.partial(far_kernel, blocks_dev),
        in_specs=[SMEM_ALL, SMEM_ALL] + [VMEM_WHOLE] * 5,
        out_specs=pl.BlockSpec(memory_space=pl.ANY),
        out_shape=jax.ShapeDtypeStruct(queries.shape, jnp.bfloat16),
        scratch_shapes=[
            pltpu.VMEM((2 * FAR_ROWS, 2 * head_dim), jnp.bfloat16),
            pltpu.VMEM((units, heads, BLK, head_dim), jnp.bfloat16),
            pltpu.SemaphoreType.DMA((units,)),
        ],
        compiler_params=limit(24),
        name="attend_far",
    )(place, table, queries, state, sums, mine, theirs)


def per_device(features, norm_gain, kv_weight, queries, step_kv, doc_ids, block_lists):
    sections = lax.axis_size("section")
    seqs = lax.axis_size("seq")
    step_total, local_heads, tok_dev, head_dim = queries.shape
    blocks_dev = tok_dev // BLK
    units = step_total * blocks_dev
    place = lax.axis_index("seq").reshape(1).astype(jnp.int32)

    partial = project(features, norm_gain, kv_weight, sections)
    parts = lax.all_to_all(partial, "section", 0, 0, tiled=True)
    lists = lax.dynamic_slice_in_dim(block_lists, place[0] * blocks_dev, blocks_dev, 1).reshape(units, LIST)
    table = pl.pallas_call(
        functools.partial(prepare_kernel, blocks_dev),
        in_specs=[SMEM_ALL, SMEM_ALL, VMEM_WHOLE],
        out_specs=SMEM_ALL,
        out_shape=jax.ShapeDtypeStruct(((units + 1) * LINE,), jnp.int32),
        scratch_shapes=[pltpu.SMEM((block_lists.shape[1],), jnp.int32)],
        compiler_params=limit(4),
        name="prepare",
    )(place, lists, doc_ids.reshape(-1, 128))

    parts, table = lax.optimization_barrier((parts, table))
    kv_cache, kv = pl.pallas_call(
        functools.partial(reduce_kernel, float(features.shape[1] * sections)),
        out_shape=[jax.ShapeDtypeStruct((tok_dev, 2 * head_dim), jnp.bfloat16)] * 2,
        compiler_params=limit(8),
        name="reduce",
    )(parts)

    every = range(seqs)

    def along_z(x, levels):
        return lax.ppermute(x, "seq", [(i, (i + 4 * levels) % seqs) for i in every])

    def along_y(x):
        return lax.ppermute(x, "seq", [(i, i ^ 2) for i in every])

    def along_core(x):
        return lax.ppermute(x, "seq", [(i, i ^ 1) for i in every])

    def join(*arrays):
        return jnp.concatenate(arrays, axis=0)

    up1 = along_z(kv, 1)
    down1 = along_z(kv, -1)
    low, high = lax.optimization_barrier((join(kv, up1), join(kv, down1)))
    up23 = along_z(low, 2)
    down23 = along_z(high, -2)
    low_y = along_y(low)
    up4 = along_z(low[:tok_dev], 4)
    column = lax.optimization_barrier(join(up23, down23, up4))
    far = along_y(column)
    near = join(low, low_y, column)
    state, sums = attend_near(place, table, queries, step_kv, (near, along_core(near)), blocks_dev)
    far, state, sums = lax.optimization_barrier((far, state, sums))
    attended = attend_far(place, table, queries, state, sums, far, along_core(far), blocks_dev)
    return attended, kv_cache[None]


def solution(mesh):
    in_specs = (
        P("seq", "section"),
        P("section"),
        P("section", None),
        P(None, "section", "seq", None),
        P(None, "section", "seq", None),
        P(),
        P(),
    )
    out_specs = (P(None, "section", "seq", None), P("section", "seq", None))
    return jax.shard_map(per_device, mesh=mesh, in_specs=in_specs, out_specs=out_specs, check_vma=False)
```

```python
import functools
import math

import jax
import jax.numpy as jnp
from jax import lax
from jax.experimental import pallas as pl
from jax.experimental.pallas import tpu as pltpu
from jax.sharding import PartitionSpec as P

HEAD = 128
BLK = 64
LIST = 16
DOCS = 8
HIDDEN = -1e30
FAR = 1 << 24
EXTRA = 8
CHUNK = 128
CLOSE = 512
RISING = 384
FALLING = 256
NEAR_ROWS = CLOSE + RISING + 2 * FALLING
FAR_ROWS = RISING
LINE = 128
COUNTS = 64
NEAR_SIZES = (4, 8, 12, 16)
FAR_SIZES = (0, 2, 4, 6, 8, 16)

VMEM_ALL = 60 << 20


def project_kernel(feat_hbm, gain_hbm, weight_hbm, out, feat, gain, weight, sems):
    tokens = feat.shape[0]
    blocks, _, width = weight.shape
    small = [
        pltpu.make_async_copy(feat_hbm, feat, sems.at[blocks]),
        pltpu.make_async_copy(gain_hbm, gain, sems.at[blocks + 1]),
    ]
    copies = [
        pltpu.make_async_copy(weight_hbm.at[:, pl.ds(j * width, width)], weight.at[j], sems.at[j]) for j in range(blocks)
    ]
    for copy in small + copies:
        copy.start()
    for copy in small:
        copy.wait()
    x = feat[...].astype(jnp.float32)
    g = x * gain[...]
    high = g.astype(jnp.bfloat16)
    both = jnp.concatenate([high, (g - high.astype(jnp.float32)).astype(jnp.bfloat16)], axis=0)
    total = jnp.sum(x * x, axis=1, keepdims=True)
    row = jnp.broadcast_to(total, (tokens, 128)).T[:EXTRA]
    top = row.astype(jnp.bfloat16).astype(jnp.float32)
    which = lax.broadcasted_iota(jnp.int32, (EXTRA, 128), 0)
    tail = jnp.where(which == 0, top, jnp.where(which == 1, row - top, 0.0)).astype(jnp.bfloat16)
    cols = out.shape[2]
    for h in range(out.shape[0]):
        out[h, tokens:, :128] = tail
        out[h, tokens:, 128:] = jnp.zeros_like(tail)
    for j, copy in enumerate(copies):
        copy.wait()
        product = jnp.dot(both, weight[j], preferred_element_type=jnp.float32)
        product = (product[:tokens] + product[tokens:]).astype(jnp.bfloat16)
        for i in range(width // cols):
            out[j * (width // cols) + i, :tokens, :] = product[:, i * cols : (i + 1) * cols]


def project(features, norm_gain, kv_weight, heads):
    tokens, width = features.shape
    cols = kv_weight.shape[1] // heads
    blocks = 4
    anywhere = pl.BlockSpec(memory_space=pl.ANY)
    return pl.pallas_call(
        project_kernel,
        in_specs=[anywhere] * 3,
        out_specs=pl.BlockSpec(memory_space=pltpu.VMEM),
        out_shape=jax.ShapeDtypeStruct((heads, tokens + EXTRA, cols), jnp.bfloat16),
        scratch_shapes=[
            pltpu.VMEM((tokens, width), features.dtype),
            pltpu.VMEM((1, width), norm_gain.dtype),
            pltpu.VMEM((blocks, width, kv_weight.shape[1] // blocks), kv_weight.dtype),
            pltpu.SemaphoreType.DMA((blocks + 2,)),
        ],
        compiler_params=pltpu.CompilerParams(vmem_limit_bytes=VMEM_ALL),
        name="project",
    )(features, norm_gain.reshape(1, width), kv_weight)


def reduce_kernel(width, parts, out, work):
    tokens = out.shape[0]
    total = jnp.sum(parts[:, tokens:, :128].astype(jnp.float32), axis=0)
    squares = jnp.broadcast_to(total[0:1] + total[1:2], (128, tokens)).T
    inverse = lax.rsqrt(squares / width + 1e-05)
    for half in range(2):
        cols = slice(half * 128, half * 128 + 128)
        kept = parts[0, :tokens, cols].astype(jnp.float32)
        for s in range(1, parts.shape[0]):
            kept = kept + parts[s, :tokens, cols].astype(jnp.float32)
        kept = (kept * inverse).astype(jnp.bfloat16)
        out[:, cols] = kept
        work[:, cols] = kept


def prepare_kernel(blocks_dev, place, lists, docs, table, seen):
    t = place[0]
    z = t // 4
    low = lax.rem(t, 4)
    units = lists.shape[0]
    d = docs[...]
    starts = [0] + [jnp.sum((d < doc).astype(jnp.int32)) for doc in range(1, DOCS)]
    for doc in range(DOCS):
        table[units * LINE + doc] = starts[doc]
    for c in range(seen.shape[0]):
        seen[c] = -1

    def unit_lists(u, carry):
        block = t * blocks_dev + lax.rem(u, blocks_dev)
        first = block * BLK
        begin = 0
        for doc in range(1, DOCS):
            begin = jnp.where(starts[doc] <= first, starts[doc], begin)
        least = begin // BLK
        base = u * LINE
        for e in range(LIST):
            table[base + e] = 0
            table[base + LIST + e] = FAR
            table[base + 2 * LIST + e] = 0
            table[base + 3 * LIST + e] = FAR
        near = 0
        far = 0
        for e in range(LIST):
            c = lists[u, e]
            keep = (c >= least) & (seen[c] != u)
            seen[c] = u
            away = z - c // 8
            x = lax.rem(c // 2, 4) ^ low
            inner = lax.rem(c, 2) * BLK
            y = x >> 1
            core = x & 1
            is_near = (away <= 1) | (y == 0) | (away >= 5)
            near_row = jnp.where(
                away <= 1,
                y * (CLOSE // 2) + away * CHUNK,
                jnp.where(away <= 4, CLOSE + (away - 2) * CHUNK, CLOSE + RISING + y * FALLING + (6 - away) * CHUNK),
            )
            near_row += core * NEAR_ROWS + inner
            far_row = core * FAR_ROWS + (away - 2) * CHUNK + inner
            at = base + jnp.where(is_near, near, 2 * LIST + far)
            row = jnp.where(is_near, near_row, far_row)
            table[at] = jnp.where(keep, row, 0)
            table[at + LIST] = jnp.where(keep, c * BLK, FAR)
            near = near + (keep & is_near).astype(jnp.int32)
            far = far + (keep & ~is_near).astype(jnp.int32)
        counts = units * LINE + COUNTS + u
        table[counts] = near
        table[counts + units] = far
        return carry

    lax.fori_loop(0, units, unit_lists, 0)


def scores(blocks, base, block, extra, begins, table, queries, held):
    pieces = [held[pl.ds(pl.multiple_of(table[base + e], BLK), BLK), :] for e in range(blocks)]
    pieces += [rows for rows, _ in extra]
    kv = jnp.concatenate(pieces, axis=0)
    lane = lax.rem(lax.broadcasted_iota(jnp.int32, (1, 128), 1), BLK)
    sub = lax.broadcasted_iota(jnp.int32, (BLK, 128), 0)
    pos_i = block * BLK + lane
    masks = []
    for e in range(blocks):
        pos_j = table[base + LIST + e] + sub
        masks.append((pos_j >= begins) & (pos_j <= pos_i))
    masks += [(sub == lane) & allowed for _, allowed in extra]
    mask = jnp.concatenate(masks, axis=0)
    mask = jnp.concatenate([mask] * (queries.shape[0] // 128), axis=1)
    s = lax.dot_general(kv[:, :HEAD], queries, (((1,), (1,)), ((), ())), preferred_element_type=jnp.float32)
    return jnp.where(mask, s, HIDDEN), kv[:, HEAD:]


def weigh(p, values):
    return lax.dot_general(
        values, p.astype(jnp.bfloat16), (((0,), (0,)), ((), ())), preferred_element_type=jnp.float32
    )


def unit_state(blocks_dev, u, t, table, q):
    steps, heads, tokens, head_dim = q.shape
    units = steps * blocks_dev
    k = u // blocks_dev
    half = lax.rem(u, blocks_dev)
    block = t * blocks_dev + half
    rows = pl.ds(pl.multiple_of(half * BLK, BLK), BLK)
    queries = q[k, :, rows, :].reshape(heads * BLK, head_dim)
    pos_i = block * BLK + lax.rem(lax.broadcasted_iota(jnp.int32, (1, 128), 1), BLK)
    begins = jnp.zeros((1, 128), jnp.int32)
    for doc in range(1, DOCS):
        start = table[units * LINE + doc]
        begins = jnp.where(start <= pos_i, start, begins)
    return k, block, rows, queries, begins


def per_size(sizes, n, run):
    least = -1
    for size in sizes:
        pl.when((n > least) & (n <= size))(functools.partial(run, size))
        least = size


SCALE = math.log2(math.e) / math.sqrt(HEAD)


def hold(held, parts):
    row = 0
    for part in parts:
        held[row : row + part.shape[0]] = part[...]
        row += part.shape[0]


def near_kernel(blocks_dev, place, table, q, own, mine, theirs, state, sums, held):
    t = place[0]
    units = q.shape[0] * blocks_dev
    hold(held, (mine, theirs))

    def body(u, carry):
        k, block, rows, queries, begins = unit_state(blocks_dev, u, t, table, q)

        def run(size):
            extra = [(own[m, 0, rows, :], m <= k) for m in range(own.shape[0])]
            s, values = scores(size, u * LINE, block, extra, begins, table, queries, held)
            top = jnp.max(s, axis=0, keepdims=True)
            p = jnp.exp2((s - top) * SCALE)
            sums[u, 0:1] = top
            sums[u, 1:2] = jnp.sum(p, axis=0, keepdims=True)
            state[u] = weigh(p, values)

        per_size(NEAR_SIZES, table[units * LINE + COUNTS + u], run)
        return carry

    lax.fori_loop(0, units, body, 0)


def far_kernel(blocks_dev, place, table, q, state, sums, mine, theirs, out, held, result, sems):
    t = place[0]
    steps, heads, tokens, head_dim = q.shape
    units = steps * blocks_dev
    hold(held, (mine, theirs))

    def copy(u):
        rows = pl.ds(pl.multiple_of(lax.rem(u, blocks_dev) * BLK, BLK), BLK)
        return pltpu.make_async_copy(result.at[u], out.at[u // blocks_dev, :, rows, :], sems.at[u])

    def body(u, carry):
        k, block, rows, queries, begins = unit_state(blocks_dev, u, t, table, q)

        def run(size):
            top, total, summed = sums[u, 0:1], sums[u, 1:2], state[u]
            if size:
                s, values = scores(size, u * LINE + 2 * LIST, block, [], begins, table, queries, held)
                new_top = jnp.maximum(top, jnp.max(s, axis=0, keepdims=True))
                p = jnp.exp2((s - new_top) * SCALE)
                factor = jnp.exp2((top - new_top) * SCALE)
                total = total * factor + jnp.sum(p, axis=0, keepdims=True)
                summed = summed * factor + weigh(p, values)
            result[u] = (summed * (1.0 / total)).T.astype(jnp.bfloat16).reshape(heads, BLK, head_dim)

        per_size(FAR_SIZES, table[units * LINE + COUNTS + units + u], run)
        copy(u).start()
        return carry

    lax.fori_loop(0, units, body, 0)
    lax.fori_loop(0, units, lambda u, c: (copy(u).wait(), c)[1], 0)


SMEM_ALL = pl.BlockSpec(memory_space=pltpu.SMEM)
VMEM_WHOLE = pl.BlockSpec(memory_space=pltpu.VMEM)


def limit(mib):
    return pltpu.CompilerParams(vmem_limit_bytes=mib << 20)


def attend_near(place, table, queries, step_kv, parts, blocks_dev):
    steps, heads, tokens, head_dim = queries.shape
    units = steps * blocks_dev
    return pl.pallas_call(
        functools.partial(near_kernel, blocks_dev),
        in_specs=[SMEM_ALL, SMEM_ALL] + [VMEM_WHOLE] * (2 + len(parts)),
        out_specs=[VMEM_WHOLE, VMEM_WHOLE],
        out_shape=[
            jax.ShapeDtypeStruct((units, head_dim, heads * BLK), jnp.float32),
            jax.ShapeDtypeStruct((units, 8, heads * BLK), jnp.float32),
        ],
        scratch_shapes=[pltpu.VMEM((2 * NEAR_ROWS, 2 * head_dim), jnp.bfloat16)],
        compiler_params=limit(24),
        name="attend_near",
    )(place, table, queries, step_kv, *parts)


def attend_far(place, table, queries, state, sums, mine, theirs, blocks_dev):
    steps, heads, tokens, head_dim = queries.shape
    units = steps * blocks_dev
    return pl.pallas_call(
        functools.partial(far_kernel, blocks_dev),
        in_specs=[SMEM_ALL, SMEM_ALL] + [VMEM_WHOLE] * 5,
        out_specs=pl.BlockSpec(memory_space=pl.ANY),
        out_shape=jax.ShapeDtypeStruct(queries.shape, jnp.bfloat16),
        scratch_shapes=[
            pltpu.VMEM((2 * FAR_ROWS, 2 * head_dim), jnp.bfloat16),
            pltpu.VMEM((units, heads, BLK, head_dim), jnp.bfloat16),
            pltpu.SemaphoreType.DMA((units,)),
        ],
        compiler_params=limit(24),
        name="attend_far",
    )(place, table, queries, state, sums, mine, theirs)


def per_device(features, norm_gain, kv_weight, queries, step_kv, doc_ids, block_lists):
    sections = lax.axis_size("section")
    seqs = lax.axis_size("seq")
    step_total, local_heads, tok_dev, head_dim = queries.shape
    blocks_dev = tok_dev // BLK
    units = step_total * blocks_dev
    place = lax.axis_index("seq").reshape(1).astype(jnp.int32)

    partial = project(features, norm_gain, kv_weight, sections)
    parts = lax.all_to_all(partial, "section", 0, 0, tiled=True)
    lists = lax.dynamic_slice_in_dim(block_lists, place[0] * blocks_dev, blocks_dev, 1).reshape(units, LIST)
    table = pl.pallas_call(
        functools.partial(prepare_kernel, blocks_dev),
        in_specs=[SMEM_ALL, SMEM_ALL, VMEM_WHOLE],
        out_specs=SMEM_ALL,
        out_shape=jax.ShapeDtypeStruct(((units + 1) * LINE,), jnp.int32),
        scratch_shapes=[pltpu.SMEM((block_lists.shape[1],), jnp.int32)],
        compiler_params=limit(4),
        name="prepare",
    )(place, lists, doc_ids.reshape(-1, 128))

    parts, table = lax.optimization_barrier((parts, table))
    kv_cache, kv = pl.pallas_call(
        functools.partial(reduce_kernel, float(features.shape[1] * sections)),
        out_shape=[jax.ShapeDtypeStruct((tok_dev, 2 * head_dim), jnp.bfloat16)] * 2,
        compiler_params=limit(8),
        name="reduce",
    )(parts)

    every = range(seqs)

    def along_z(x, levels):
        return lax.ppermute(x, "seq", [(i, (i + 4 * levels) % seqs) for i in every])

    def along_y(x):
        return lax.ppermute(x, "seq", [(i, i ^ 2) for i in every])

    def along_core(x):
        return lax.ppermute(x, "seq", [(i, i ^ 1) for i in every])

    def join(*arrays):
        return jnp.concatenate(arrays, axis=0)

    up1 = along_z(kv, 1)
    down1 = along_z(kv, -1)
    low, high = lax.optimization_barrier((join(kv, up1), join(kv, down1)))
    down23 = along_z(high, -2)
    up23 = along_z(low, 2)
    low_y = along_y(low)
    up4 = along_z(low[:tok_dev], 4)
    falling = join(down23, along_y(down23))
    rising = join(up23, up4)
    far = along_y(rising)
    near = join(low, low_y, rising, falling)
    state, sums = attend_near(place, table, queries, step_kv, (near, along_core(near)), blocks_dev)
    far, state, sums = lax.optimization_barrier((far, state, sums))
    attended = attend_far(place, table, queries, state, sums, far, along_core(far), blocks_dev)
    return attended, kv_cache[None]


def solution(mesh):
    in_specs = (
        P("seq", "section"),
        P("section"),
        P("section", None),
        P(None, "section", "seq", None),
        P(None, "section", "seq", None),
        P(),
        P(),
    )
    out_specs = (P(None, "section", "seq", None), P("section", "seq", None))
    return jax.shard_map(per_device, mesh=mesh, in_specs=in_specs, out_specs=out_specs, check_vma=False)
```

```python
import functools
import math

import jax
import jax.numpy as jnp
from jax import lax
from jax.experimental import pallas as pl
from jax.experimental.pallas import tpu as pltpu
from jax.sharding import PartitionSpec as P

HEAD = 128
BLK = 64
LIST = 16
DOCS = 8
HIDDEN = -1e30
FAR = 1 << 24
EXTRA = 8
CHUNK = 128
CLOSE = 512
RISING = 384
FALLING = 256
NEAR_ROWS = CLOSE + RISING + 2 * FALLING
FAR_ROWS = RISING
LINE = 128
COUNTS = 64
NEAR_SIZES = (2, 4, 6, 8, 10, 12, 16)
FAR_SIZES = (0, 2, 4, 6, 8, 16)

VMEM_ALL = 60 << 20


def project_kernel(feat_hbm, gain_hbm, weight_hbm, out, feat, gain, weight, sems):
    tokens = feat.shape[0]
    blocks, _, width = weight.shape
    small = [
        pltpu.make_async_copy(feat_hbm, feat, sems.at[blocks]),
        pltpu.make_async_copy(gain_hbm, gain, sems.at[blocks + 1]),
    ]
    copies = [
        pltpu.make_async_copy(weight_hbm.at[:, pl.ds(j * width, width)], weight.at[j], sems.at[j]) for j in range(blocks)
    ]
    for copy in small + copies:
        copy.start()
    for copy in small:
        copy.wait()
    x = feat[...].astype(jnp.float32)
    g = x * gain[...]
    high = g.astype(jnp.bfloat16)
    both = jnp.concatenate([high, (g - high.astype(jnp.float32)).astype(jnp.bfloat16)], axis=0)
    total = jnp.sum(x * x, axis=1, keepdims=True)
    row = jnp.broadcast_to(total, (tokens, 128)).T[:EXTRA]
    top = row.astype(jnp.bfloat16).astype(jnp.float32)
    which = lax.broadcasted_iota(jnp.int32, (EXTRA, 128), 0)
    tail = jnp.where(which == 0, top, jnp.where(which == 1, row - top, 0.0)).astype(jnp.bfloat16)
    cols = out.shape[2]
    for h in range(out.shape[0]):
        out[h, tokens:, :128] = tail
        out[h, tokens:, 128:] = jnp.zeros_like(tail)
    for j, copy in enumerate(copies):
        copy.wait()
        product = jnp.dot(both, weight[j], preferred_element_type=jnp.float32)
        product = (product[:tokens] + product[tokens:]).astype(jnp.bfloat16)
        for i in range(width // cols):
            out[j * (width // cols) + i, :tokens, :] = product[:, i * cols : (i + 1) * cols]


def project(features, norm_gain, kv_weight, heads):
    tokens, width = features.shape
    cols = kv_weight.shape[1] // heads
    blocks = 8
    anywhere = pl.BlockSpec(memory_space=pl.ANY)
    return pl.pallas_call(
        project_kernel,
        in_specs=[anywhere] * 3,
        out_specs=pl.BlockSpec(memory_space=pltpu.VMEM),
        out_shape=jax.ShapeDtypeStruct((heads, tokens + EXTRA, cols), jnp.bfloat16),
        scratch_shapes=[
            pltpu.VMEM((tokens, width), features.dtype),
            pltpu.VMEM((1, width), norm_gain.dtype),
            pltpu.VMEM((blocks, width, kv_weight.shape[1] // blocks), kv_weight.dtype),
            pltpu.SemaphoreType.DMA((blocks + 2,)),
        ],
        compiler_params=pltpu.CompilerParams(vmem_limit_bytes=VMEM_ALL),
        name="project",
    )(features, norm_gain.reshape(1, width), kv_weight)


def reduce_kernel(width, parts, out, work):
    tokens = out.shape[0]
    total = jnp.sum(parts[:, tokens:, :128].astype(jnp.float32), axis=0)
    squares = jnp.broadcast_to(total[0:1] + total[1:2], (128, tokens)).T
    inverse = lax.rsqrt(squares / width + 1e-05)
    for half in range(2):
        cols = slice(half * 128, half * 128 + 128)
        kept = parts[0, :tokens, cols].astype(jnp.float32)
        for s in range(1, parts.shape[0]):
            kept = kept + parts[s, :tokens, cols].astype(jnp.float32)
        kept = (kept * inverse).astype(jnp.bfloat16)
        out[:, cols] = kept
        work[:, cols] = kept


def prepare_kernel(blocks_dev, place, lists, docs, table, seen):
    t = place[0]
    z = t // 4
    low = lax.rem(t, 4)
    units = lists.shape[0]
    d = docs[...]
    starts = [0] + [jnp.sum((d < doc).astype(jnp.int32)) for doc in range(1, DOCS)]
    for doc in range(DOCS):
        table[units * LINE + doc] = starts[doc]
    for c in range(seen.shape[0]):
        seen[c] = -1

    def unit_lists(u, carry):
        block = t * blocks_dev + lax.rem(u, blocks_dev)
        first = block * BLK
        begin = 0
        for doc in range(1, DOCS):
            begin = jnp.where(starts[doc] <= first, starts[doc], begin)
        least = begin // BLK
        base = u * LINE
        for e in range(LIST):
            table[base + e] = 0
            table[base + LIST + e] = FAR
            table[base + 2 * LIST + e] = 0
            table[base + 3 * LIST + e] = FAR
        near = 0
        far = 0
        for e in range(LIST):
            c = lists[u, e]
            keep = (c >= least) & (seen[c] != u)
            seen[c] = u
            away = z - c // 8
            x = lax.rem(c // 2, 4) ^ low
            inner = lax.rem(c, 2) * BLK
            y = x >> 1
            core = x & 1
            is_near = (away <= 1) | (y == 0) | (away >= 5)
            near_row = jnp.where(
                away <= 1,
                y * (CLOSE // 2) + away * CHUNK,
                jnp.where(away <= 4, CLOSE + (away - 2) * CHUNK, CLOSE + RISING + y * FALLING + (6 - away) * CHUNK),
            )
            near_row += core * NEAR_ROWS + inner
            far_row = core * FAR_ROWS + (away - 2) * CHUNK + inner
            at = base + jnp.where(is_near, near, 2 * LIST + far)
            row = jnp.where(is_near, near_row, far_row)
            table[at] = jnp.where(keep, row, 0)
            table[at + LIST] = jnp.where(keep, c * BLK, FAR)
            near = near + (keep & is_near).astype(jnp.int32)
            far = far + (keep & ~is_near).astype(jnp.int32)
        counts = units * LINE + COUNTS + u
        table[counts] = near
        table[counts + units] = far
        return carry

    lax.fori_loop(0, units, unit_lists, 0)


def scores(blocks, base, block, extra, begins, table, queries, held):
    pieces = [held[pl.ds(pl.multiple_of(table[base + e], BLK), BLK), :] for e in range(blocks)]
    pieces += [rows for rows, _ in extra]
    kv = jnp.concatenate(pieces, axis=0)
    lane = lax.rem(lax.broadcasted_iota(jnp.int32, (1, 128), 1), BLK)
    sub = lax.broadcasted_iota(jnp.int32, (BLK, 128), 0)
    pos_i = block * BLK + lane
    masks = []
    for e in range(blocks):
        pos_j = table[base + LIST + e] + sub
        masks.append((pos_j >= begins) & (pos_j <= pos_i))
    masks += [(sub == lane) & allowed for _, allowed in extra]
    mask = jnp.concatenate(masks, axis=0)
    mask = jnp.concatenate([mask] * (queries.shape[0] // 128), axis=1)
    s = lax.dot_general(kv[:, :HEAD], queries, (((1,), (1,)), ((), ())), preferred_element_type=jnp.float32)
    return jnp.where(mask, s, HIDDEN), kv[:, HEAD:]


def weigh(p, values):
    return lax.dot_general(
        values, p.astype(jnp.bfloat16), (((0,), (0,)), ((), ())), preferred_element_type=jnp.float32
    )


def unit_state(blocks_dev, u, t, table, q):
    steps, heads, tokens, head_dim = q.shape
    units = steps * blocks_dev
    k = u // blocks_dev
    half = lax.rem(u, blocks_dev)
    block = t * blocks_dev + half
    rows = pl.ds(pl.multiple_of(half * BLK, BLK), BLK)
    queries = q[k, :, rows, :].reshape(heads * BLK, head_dim)
    pos_i = block * BLK + lax.rem(lax.broadcasted_iota(jnp.int32, (1, 128), 1), BLK)
    begins = jnp.zeros((1, 128), jnp.int32)
    for doc in range(1, DOCS):
        start = table[units * LINE + doc]
        begins = jnp.where(start <= pos_i, start, begins)
    return k, block, rows, queries, begins


def per_size(sizes, n, run):
    least = -1
    for size in sizes:
        pl.when((n > least) & (n <= size))(functools.partial(run, size))
        least = size


SCALE = math.log2(math.e) / math.sqrt(HEAD)


def hold(held, parts):
    row = 0
    for part in parts:
        held[row : row + part.shape[0]] = part[...]
        row += part.shape[0]


def own_kernel(blocks_dev, q, own, state, sums):
    steps, heads, tokens, head_dim = q.shape

    def body(u, carry):
        k = u // blocks_dev
        rows = pl.ds(pl.multiple_of(lax.rem(u, blocks_dev) * BLK, BLK), BLK)
        queries = q[k, :, rows, :].reshape(heads * BLK, head_dim)
        extra = [(own[m, 0, rows, :], m <= k) for m in range(steps)]
        s, values = scores(0, 0, 0, extra, None, None, queries, None)
        top = jnp.max(s, axis=0, keepdims=True)
        p = jnp.exp2((s - top) * SCALE)
        sums[u, 0:1] = top
        sums[u, 1:2] = jnp.sum(p, axis=0, keepdims=True)
        state[u] = weigh(p, values)
        return carry

    lax.fori_loop(0, steps * blocks_dev, body, 0)


def add_blocks(size, u, base, block, begins, table, queries, held, state, sums):
    top, total, summed = sums[u, 0:1], sums[u, 1:2], state[u]
    if size:
        s, values = scores(size, base, block, [], begins, table, queries, held)
        new_top = jnp.maximum(top, jnp.max(s, axis=0, keepdims=True))
        p = jnp.exp2((s - new_top) * SCALE)
        factor = jnp.exp2((top - new_top) * SCALE)
        total = total * factor + jnp.sum(p, axis=0, keepdims=True)
        summed = summed * factor + weigh(p, values)
        top = new_top
    return top, total, summed


def near_kernel(blocks_dev, place, table, q, old_state, old_sums, mine, theirs, state, sums, held):
    t = place[0]
    units = q.shape[0] * blocks_dev
    hold(held, (mine, theirs))

    def body(u, carry):
        k, block, rows, queries, begins = unit_state(blocks_dev, u, t, table, q)

        def run(size):
            top, total, summed = add_blocks(
                size, u, u * LINE, block, begins, table, queries, held, old_state, old_sums
            )
            sums[u, 0:1] = top
            sums[u, 1:2] = total
            state[u] = summed

        per_size(NEAR_SIZES, table[units * LINE + COUNTS + u], run)
        return carry

    lax.fori_loop(0, units, body, 0)


def far_kernel(blocks_dev, place, table, q, state, sums, mine, theirs, out, held, result, sems):
    t = place[0]
    steps, heads, tokens, head_dim = q.shape
    units = steps * blocks_dev
    hold(held, (mine, theirs))

    def copy(u):
        rows = pl.ds(pl.multiple_of(lax.rem(u, blocks_dev) * BLK, BLK), BLK)
        return pltpu.make_async_copy(result.at[u], out.at[u // blocks_dev, :, rows, :], sems.at[u])

    def body(u, carry):
        k, block, rows, queries, begins = unit_state(blocks_dev, u, t, table, q)

        def run(size):
            top, total, summed = add_blocks(
                size, u, u * LINE + 2 * LIST, block, begins, table, queries, held, state, sums
            )
            result[u] = (summed * (1.0 / total)).T.astype(jnp.bfloat16).reshape(heads, BLK, head_dim)

        per_size(FAR_SIZES, table[units * LINE + COUNTS + units + u], run)
        copy(u).start()
        return carry

    lax.fori_loop(0, units, body, 0)
    lax.fori_loop(0, units, lambda u, c: (copy(u).wait(), c)[1], 0)


SMEM_ALL = pl.BlockSpec(memory_space=pltpu.SMEM)
VMEM_WHOLE = pl.BlockSpec(memory_space=pltpu.VMEM)


def limit(mib):
    return pltpu.CompilerParams(vmem_limit_bytes=mib << 20)


def state_shapes(queries, blocks_dev):
    steps, heads, tokens, head_dim = queries.shape
    units = steps * blocks_dev
    return [
        jax.ShapeDtypeStruct((units, head_dim, heads * BLK), jnp.float32),
        jax.ShapeDtypeStruct((units, 8, heads * BLK), jnp.float32),
    ]


def attend_own(queries, step_kv, blocks_dev):
    return pl.pallas_call(
        functools.partial(own_kernel, blocks_dev),
        in_specs=[VMEM_WHOLE] * 2,
        out_specs=[VMEM_WHOLE] * 2,
        out_shape=state_shapes(queries, blocks_dev),
        compiler_params=limit(16),
        name="attend_own",
    )(queries, step_kv)


def attend_near(place, table, queries, state, sums, mine, theirs, blocks_dev):
    return pl.pallas_call(
        functools.partial(near_kernel, blocks_dev),
        in_specs=[SMEM_ALL] * 2 + [VMEM_WHOLE] * 5,
        out_specs=[VMEM_WHOLE] * 2,
        out_shape=state_shapes(queries, blocks_dev),
        input_output_aliases={3: 0, 4: 1},
        scratch_shapes=[pltpu.VMEM((2 * NEAR_ROWS, mine.shape[1]), jnp.bfloat16)],
        compiler_params=limit(24),
        name="attend_near",
    )(place, table, queries, state, sums, mine, theirs)


def attend_far(place, table, queries, state, sums, mine, theirs, blocks_dev):
    steps, heads, tokens, head_dim = queries.shape
    units = steps * blocks_dev
    return pl.pallas_call(
        functools.partial(far_kernel, blocks_dev),
        in_specs=[SMEM_ALL, SMEM_ALL] + [VMEM_WHOLE] * 5,
        out_specs=pl.BlockSpec(memory_space=pl.ANY),
        out_shape=jax.ShapeDtypeStruct(queries.shape, jnp.bfloat16),
        scratch_shapes=[
            pltpu.VMEM((2 * FAR_ROWS, 2 * head_dim), jnp.bfloat16),
            pltpu.VMEM((units, heads, BLK, head_dim), jnp.bfloat16),
            pltpu.SemaphoreType.DMA((units,)),
        ],
        compiler_params=limit(24),
        name="attend_far",
    )(place, table, queries, state, sums, mine, theirs)


def per_device(features, norm_gain, kv_weight, queries, step_kv, doc_ids, block_lists):
    sections = lax.axis_size("section")
    seqs = lax.axis_size("seq")
    step_total, local_heads, tok_dev, head_dim = queries.shape
    blocks_dev = tok_dev // BLK
    units = step_total * blocks_dev
    place = lax.axis_index("seq").reshape(1).astype(jnp.int32)

    partial = project(features, norm_gain, kv_weight, sections)
    parts = lax.all_to_all(partial, "section", 0, 0, tiled=True)
    lists = lax.dynamic_slice_in_dim(block_lists, place[0] * blocks_dev, blocks_dev, 1).reshape(units, LIST)
    table = pl.pallas_call(
        functools.partial(prepare_kernel, blocks_dev),
        in_specs=[SMEM_ALL, SMEM_ALL, VMEM_WHOLE],
        out_specs=SMEM_ALL,
        out_shape=jax.ShapeDtypeStruct(((units + 1) * LINE,), jnp.int32),
        scratch_shapes=[pltpu.SMEM((block_lists.shape[1],), jnp.int32)],
        compiler_params=limit(4),
        name="prepare",
    )(place, lists, doc_ids.reshape(-1, 128))

    state, sums = attend_own(queries, step_kv, blocks_dev)
    parts, table, state, sums = lax.optimization_barrier((parts, table, state, sums))
    kv_cache, kv = pl.pallas_call(
        functools.partial(reduce_kernel, float(features.shape[1] * sections)),
        out_shape=[jax.ShapeDtypeStruct((tok_dev, 2 * head_dim), jnp.bfloat16)] * 2,
        compiler_params=limit(8),
        name="reduce",
    )(parts)

    every = range(seqs)

    def along_z(x, levels):
        return lax.ppermute(x, "seq", [(i, (i + 4 * levels) % seqs) for i in every])

    def along_y(x):
        return lax.ppermute(x, "seq", [(i, i ^ 2) for i in every])

    def along_core(x):
        return lax.ppermute(x, "seq", [(i, i ^ 1) for i in every])

    def join(*arrays):
        return jnp.concatenate(arrays, axis=0)

    up1 = along_z(kv, 1)
    down1 = along_z(kv, -1)
    low, high = lax.optimization_barrier((join(kv, up1), join(kv, down1)))
    down23 = along_z(high, -2)
    up23 = along_z(low, 2)
    low_y = along_y(low)
    up4 = along_z(low[:tok_dev], 4)
    falling = join(down23, along_y(down23))
    rising = join(up23, up4)
    far = along_y(rising)
    near = join(low, low_y, rising, falling)
    state, sums = attend_near(place, table, queries, state, sums, near, along_core(near), blocks_dev)
    far, state, sums = lax.optimization_barrier((far, state, sums))
    attended = attend_far(place, table, queries, state, sums, far, along_core(far), blocks_dev)
    return attended, kv_cache[None]


def solution(mesh):
    in_specs = (
        P("seq", "section"),
        P("section"),
        P("section", None),
        P(None, "section", "seq", None),
        P(None, "section", "seq", None),
        P(),
        P(),
    )
    out_specs = (P(None, "section", "seq", None), P("section", "seq", None))
    return jax.shard_map(per_device, mesh=mesh, in_specs=in_specs, out_specs=out_specs, check_vma=False)
```

```python
import functools
import math

import jax
import jax.numpy as jnp
from jax import lax
from jax.experimental import pallas as pl
from jax.experimental.pallas import tpu as pltpu
from jax.sharding import PartitionSpec as P

HEAD = 128
BLK = 64
LIST = 16
DOCS = 8
HIDDEN = -1e30
FAR = 1 << 24
EXTRA = 8
CHUNK = 128
CLOSE = 512
RISING = 384
FALLING = 256
NEAR_ROWS = CLOSE + RISING + 2 * FALLING
FAR_ROWS = RISING
LINE = 128
COUNTS = 64
NEAR_SIZES = (2, 4, 6, 8, 10, 12, 16)
FAR_SIZES = (0, 2, 4, 6, 8, 16)


def project_kernel(feat_hbm, gain_hbm, weight_hbm, out, feat, gain, weight, sems):
    tokens = feat.shape[0]
    blocks, _, width = weight.shape
    small = [
        pltpu.make_async_copy(feat_hbm, feat, sems.at[blocks]),
        pltpu.make_async_copy(gain_hbm, gain, sems.at[blocks + 1]),
    ]
    copies = [
        pltpu.make_async_copy(weight_hbm.at[:, pl.ds(j * width, width)], weight.at[j], sems.at[j]) for j in range(blocks)
    ]
    for copy in small + copies:
        copy.start()
    for copy in small:
        copy.wait()
    x = feat[...].astype(jnp.float32)
    g = x * gain[...]
    high = g.astype(jnp.bfloat16)
    both = jnp.concatenate([high, (g - high.astype(jnp.float32)).astype(jnp.bfloat16)], axis=0)
    total = jnp.sum(x * x, axis=1, keepdims=True)
    row = jnp.broadcast_to(total, (tokens, 128)).T[:EXTRA]
    top = row.astype(jnp.bfloat16).astype(jnp.float32)
    which = lax.broadcasted_iota(jnp.int32, (EXTRA, 128), 0)
    tail = jnp.where(which == 0, top, jnp.where(which == 1, row - top, 0.0)).astype(jnp.bfloat16)
    cols = out.shape[2]
    for h in range(out.shape[0]):
        out[h, tokens:, :128] = tail
        out[h, tokens:, 128:] = jnp.zeros_like(tail)
    for j, copy in enumerate(copies):
        copy.wait()
        product = jnp.dot(both, weight[j], preferred_element_type=jnp.float32)
        product = (product[:tokens] + product[tokens:]).astype(jnp.bfloat16)
        for i in range(width // cols):
            out[j * (width // cols) + i, :tokens, :] = product[:, i * cols : (i + 1) * cols]


def project(features, norm_gain, kv_weight, heads):
    tokens, width = features.shape
    cols = kv_weight.shape[1] // heads
    blocks = 4
    anywhere = pl.BlockSpec(memory_space=pl.ANY)
    return pl.pallas_call(
        project_kernel,
        in_specs=[anywhere] * 3,
        out_specs=pl.BlockSpec(memory_space=pltpu.VMEM),
        out_shape=jax.ShapeDtypeStruct((heads, tokens + EXTRA, cols), jnp.bfloat16),
        scratch_shapes=[
            pltpu.VMEM((tokens, width), features.dtype),
            pltpu.VMEM((1, width), norm_gain.dtype),
            pltpu.VMEM((blocks, width, kv_weight.shape[1] // blocks), kv_weight.dtype),
            pltpu.SemaphoreType.DMA((blocks + 2,)),
        ],
        compiler_params=pltpu.CompilerParams(vmem_limit_bytes=60 << 20),
        name="project",
    )(features, norm_gain.reshape(1, width), kv_weight)


def reduce_kernel(width, parts, out, work):
    tokens = out.shape[0]
    total = jnp.sum(parts[:, tokens:, :128].astype(jnp.float32), axis=0)
    squares = jnp.broadcast_to(total[0:1] + total[1:2], (128, tokens)).T
    inverse = lax.rsqrt(squares / width + 1e-05)
    for half in range(2):
        cols = slice(half * 128, half * 128 + 128)
        kept = parts[0, :tokens, cols].astype(jnp.float32)
        for s in range(1, parts.shape[0]):
            kept = kept + parts[s, :tokens, cols].astype(jnp.float32)
        kept = (kept * inverse).astype(jnp.bfloat16)
        out[:, cols] = kept
        work[:, cols] = kept


def prepare_kernel(blocks_dev, place, lists, docs, table, seen):
    t = place[0]
    z = t // 4
    low = lax.rem(t, 4)
    units = lists.shape[0]
    d = docs[...]
    starts = [0] + [jnp.sum((d < doc).astype(jnp.int32)) for doc in range(1, DOCS)]
    for doc in range(DOCS):
        table[units * LINE + doc] = starts[doc]
    for c in range(seen.shape[0]):
        seen[c] = -1

    def unit_lists(u, carry):
        block = t * blocks_dev + lax.rem(u, blocks_dev)
        first = block * BLK
        begin = 0
        for doc in range(1, DOCS):
            begin = jnp.where(starts[doc] <= first, starts[doc], begin)
        least = begin // BLK
        base = u * LINE
        for e in range(LIST):
            table[base + e] = 0
            table[base + LIST + e] = FAR
            table[base + 2 * LIST + e] = 0
            table[base + 3 * LIST + e] = FAR
        near = 0
        far = 0
        for e in range(LIST):
            c = lists[u, e]
            keep = (c >= least) & (seen[c] != u)
            seen[c] = u
            away = z - c // 8
            x = lax.rem(c // 2, 4) ^ low
            inner = lax.rem(c, 2) * BLK
            y = x >> 1
            core = x & 1
            is_near = (away <= 1) | (y == 0) | (away >= 5)
            near_row = jnp.where(
                away <= 1,
                y * (CLOSE // 2) + away * CHUNK,
                jnp.where(away <= 4, CLOSE + (away - 2) * CHUNK, CLOSE + RISING + y * FALLING + (6 - away) * CHUNK),
            )
            near_row += core * NEAR_ROWS + inner
            far_row = core * FAR_ROWS + (away - 2) * CHUNK + inner
            at = base + jnp.where(is_near, near, 2 * LIST + far)
            row = jnp.where(is_near, near_row, far_row)
            table[at] = jnp.where(keep, row, 0)
            table[at + LIST] = jnp.where(keep, c * BLK, FAR)
            near = near + (keep & is_near).astype(jnp.int32)
            far = far + (keep & ~is_near).astype(jnp.int32)
        counts = units * LINE + COUNTS + u
        table[counts] = near
        table[counts + units] = far
        return carry

    lax.fori_loop(0, units, unit_lists, 0)


def scores(blocks, base, block, extra, begins, table, queries, held):
    pieces = [held[pl.ds(pl.multiple_of(table[base + e], BLK), BLK), :] for e in range(blocks)]
    pieces += [rows for rows, _ in extra]
    kv = jnp.concatenate(pieces, axis=0)
    lane = lax.rem(lax.broadcasted_iota(jnp.int32, (1, 128), 1), BLK)
    sub = lax.broadcasted_iota(jnp.int32, (BLK, 128), 0)
    pos_i = block * BLK + lane
    masks = []
    for e in range(blocks):
        pos_j = table[base + LIST + e] + sub
        masks.append((pos_j >= begins) & (pos_j <= pos_i))
    masks += [(sub == lane) & allowed for _, allowed in extra]
    mask = jnp.concatenate(masks, axis=0)
    mask = jnp.concatenate([mask] * (queries.shape[0] // 128), axis=1)
    s = lax.dot_general(kv[:, :HEAD], queries, (((1,), (1,)), ((), ())), preferred_element_type=jnp.float32)
    return jnp.where(mask, s, HIDDEN), kv[:, HEAD:]


def weigh(p, values):
    return lax.dot_general(
        values, p.astype(jnp.bfloat16), (((0,), (0,)), ((), ())), preferred_element_type=jnp.float32
    )


def unit_state(blocks_dev, u, t, table, q):
    steps, heads, tokens, head_dim = q.shape
    units = steps * blocks_dev
    k = u // blocks_dev
    half = lax.rem(u, blocks_dev)
    block = t * blocks_dev + half
    rows = pl.ds(pl.multiple_of(half * BLK, BLK), BLK)
    queries = q[k, :, rows, :].reshape(heads * BLK, head_dim)
    pos_i = block * BLK + lax.rem(lax.broadcasted_iota(jnp.int32, (1, 128), 1), BLK)
    begins = jnp.zeros((1, 128), jnp.int32)
    for doc in range(1, DOCS):
        start = table[units * LINE + doc]
        begins = jnp.where(start <= pos_i, start, begins)
    return k, block, rows, queries, begins


def per_size(sizes, n, run):
    least = -1
    for size in sizes:
        pl.when((n > least) & (n <= size))(functools.partial(run, size))
        least = size


SCALE = math.log2(math.e) / math.sqrt(HEAD)


def hold(held, parts):
    row = 0
    for part in parts:
        held[row : row + part.shape[0]] = part[...]
        row += part.shape[0]


def own_kernel(blocks_dev, q, own, state, sums):
    steps, heads, tokens, head_dim = q.shape

    def body(u, carry):
        k = u // blocks_dev
        rows = pl.ds(pl.multiple_of(lax.rem(u, blocks_dev) * BLK, BLK), BLK)
        queries = q[k, :, rows, :].reshape(heads * BLK, head_dim)
        extra = [(own[m, 0, rows, :], m <= k) for m in range(steps)]
        s, values = scores(0, 0, 0, extra, None, None, queries, None)
        top = jnp.max(s, axis=0, keepdims=True)
        p = jnp.exp2((s - top) * SCALE)
        sums[u, 0:1] = top
        sums[u, 1:2] = jnp.sum(p, axis=0, keepdims=True)
        state[u] = weigh(p, values)
        return carry

    lax.fori_loop(0, steps * blocks_dev, body, 0)


def add_blocks(size, u, base, block, begins, table, queries, held, state, sums):
    top, total, summed = sums[u, 0:1], sums[u, 1:2], state[u]
    if size:
        s, values = scores(size, base, block, [], begins, table, queries, held)
        new_top = jnp.maximum(top, jnp.max(s, axis=0, keepdims=True))
        p = jnp.exp2((s - new_top) * SCALE)
        factor = jnp.exp2((top - new_top) * SCALE)
        total = total * factor + jnp.sum(p, axis=0, keepdims=True)
        summed = summed * factor + weigh(p, values)
        top = new_top
    return top, total, summed


def near_kernel(blocks_dev, place, table, q, old_state, old_sums, mine, theirs, state, sums, held):
    t = place[0]
    units = q.shape[0] * blocks_dev
    hold(held, (mine, theirs))

    def body(u, carry):
        k, block, rows, queries, begins = unit_state(blocks_dev, u, t, table, q)

        def run(size):
            top, total, summed = add_blocks(
                size, u, u * LINE, block, begins, table, queries, held, old_state, old_sums
            )
            sums[u, 0:1] = top
            sums[u, 1:2] = total
            state[u] = summed

        per_size(NEAR_SIZES, table[units * LINE + COUNTS + u], run)
        return carry

    lax.fori_loop(0, units, body, 0)


def far_kernel(blocks_dev, place, table, q, state, sums, mine, theirs, out, held, result, sems):
    t = place[0]
    steps, heads, tokens, head_dim = q.shape
    units = steps * blocks_dev
    hold(held, (mine, theirs))

    def copy(u):
        rows = pl.ds(pl.multiple_of(lax.rem(u, blocks_dev) * BLK, BLK), BLK)
        return pltpu.make_async_copy(result.at[u], out.at[u // blocks_dev, :, rows, :], sems.at[u])

    def body(u, carry):
        k, block, rows, queries, begins = unit_state(blocks_dev, u, t, table, q)

        def run(size):
            top, total, summed = add_blocks(
                size, u, u * LINE + 2 * LIST, block, begins, table, queries, held, state, sums
            )
            result[u] = (summed * (1.0 / total)).T.astype(jnp.bfloat16).reshape(heads, BLK, head_dim)

        per_size(FAR_SIZES, table[units * LINE + COUNTS + units + u], run)
        copy(u).start()
        return carry

    lax.fori_loop(0, units, body, 0)
    lax.fori_loop(0, units, lambda u, c: (copy(u).wait(), c)[1], 0)


SMEM_ALL = pl.BlockSpec(memory_space=pltpu.SMEM)
VMEM_WHOLE = pl.BlockSpec(memory_space=pltpu.VMEM)


def limit(mib):
    return pltpu.CompilerParams(vmem_limit_bytes=mib << 20)


def state_shapes(queries, blocks_dev):
    steps, heads, tokens, head_dim = queries.shape
    units = steps * blocks_dev
    return [
        jax.ShapeDtypeStruct((units, head_dim, heads * BLK), jnp.float32),
        jax.ShapeDtypeStruct((units, 8, heads * BLK), jnp.float32),
    ]


def attend_own(queries, step_kv, blocks_dev):
    return pl.pallas_call(
        functools.partial(own_kernel, blocks_dev),
        in_specs=[VMEM_WHOLE] * 2,
        out_specs=[VMEM_WHOLE] * 2,
        out_shape=state_shapes(queries, blocks_dev),
        compiler_params=limit(16),
        name="attend_own",
    )(queries, step_kv)


def attend_near(place, table, queries, state, sums, mine, theirs, blocks_dev):
    return pl.pallas_call(
        functools.partial(near_kernel, blocks_dev),
        in_specs=[SMEM_ALL] * 2 + [VMEM_WHOLE] * 5,
        out_specs=[VMEM_WHOLE] * 2,
        out_shape=state_shapes(queries, blocks_dev),
        input_output_aliases={3: 0, 4: 1},
        scratch_shapes=[pltpu.VMEM((2 * NEAR_ROWS, mine.shape[1]), jnp.bfloat16)],
        compiler_params=limit(24),
        name="attend_near",
    )(place, table, queries, state, sums, mine, theirs)


def attend_far(place, table, queries, state, sums, mine, theirs, blocks_dev):
    steps, heads, tokens, head_dim = queries.shape
    units = steps * blocks_dev
    return pl.pallas_call(
        functools.partial(far_kernel, blocks_dev),
        in_specs=[SMEM_ALL, SMEM_ALL] + [VMEM_WHOLE] * 5,
        out_specs=pl.BlockSpec(memory_space=pl.ANY),
        out_shape=jax.ShapeDtypeStruct(queries.shape, jnp.bfloat16),
        scratch_shapes=[
            pltpu.VMEM((2 * FAR_ROWS, 2 * head_dim), jnp.bfloat16),
            pltpu.VMEM((units, heads, BLK, head_dim), jnp.bfloat16),
            pltpu.SemaphoreType.DMA((units,)),
        ],
        compiler_params=limit(24),
        name="attend_far",
    )(place, table, queries, state, sums, mine, theirs)


def per_device(features, norm_gain, kv_weight, queries, step_kv, doc_ids, block_lists):
    sections = lax.axis_size("section")
    seqs = lax.axis_size("seq")
    step_total, local_heads, tok_dev, head_dim = queries.shape
    blocks_dev = tok_dev // BLK
    units = step_total * blocks_dev
    place = lax.axis_index("seq").reshape(1).astype(jnp.int32)

    partial = project(features, norm_gain, kv_weight, sections)
    parts = lax.all_to_all(partial, "section", 0, 0, tiled=True)
    lists = lax.dynamic_slice_in_dim(block_lists, place[0] * blocks_dev, blocks_dev, 1).reshape(units, LIST)
    table = pl.pallas_call(
        functools.partial(prepare_kernel, blocks_dev),
        in_specs=[SMEM_ALL, SMEM_ALL, VMEM_WHOLE],
        out_specs=SMEM_ALL,
        out_shape=jax.ShapeDtypeStruct(((units + 1) * LINE,), jnp.int32),
        scratch_shapes=[pltpu.SMEM((block_lists.shape[1],), jnp.int32)],
        compiler_params=limit(4),
        name="prepare",
    )(place, lists, doc_ids.reshape(-1, 128))

    state, sums = attend_own(queries, step_kv, blocks_dev)
    parts, table, state, sums = lax.optimization_barrier((parts, table, state, sums))
    kv_cache, kv = pl.pallas_call(
        functools.partial(reduce_kernel, float(features.shape[1] * sections)),
        out_shape=[jax.ShapeDtypeStruct((tok_dev, 2 * head_dim), jnp.bfloat16)] * 2,
        compiler_params=limit(8),
        name="reduce",
    )(parts)

    every = range(seqs)

    def along_z(x, levels):
        return lax.ppermute(x, "seq", [(i, (i + 4 * levels) % seqs) for i in every])

    def along_y(x):
        return lax.ppermute(x, "seq", [(i, i ^ 2) for i in every])

    def along_core(x):
        return lax.ppermute(x, "seq", [(i, i ^ 1) for i in every])

    def join(*arrays):
        return jnp.concatenate(arrays, axis=0)

    up1 = along_z(kv, 1)
    down1 = along_z(kv, -1)
    low, high = lax.optimization_barrier((join(kv, up1), join(kv, down1)))
    down23 = along_z(high, -2)
    up23 = along_z(low, 2)
    low_y = along_y(low)
    up4 = along_z(high[tok_dev:], -3)
    falling = join(down23, along_y(down23))
    rising = join(up23, up4)
    far = along_y(rising)
    near = join(low, low_y, rising, falling)
    state, sums = attend_near(place, table, queries, state, sums, near, along_core(near), blocks_dev)
    far, state, sums = lax.optimization_barrier((far, state, sums))
    attended = attend_far(place, table, queries, state, sums, far, along_core(far), blocks_dev)
    return attended, kv_cache[None]


def solution(mesh):
    in_specs = (
        P("seq", "section"),
        P("section"),
        P("section", None),
        P(None, "section", "seq", None),
        P(None, "section", "seq", None),
        P(),
        P(),
    )
    out_specs = (P(None, "section", "seq", None), P("section", "seq", None))
    return jax.shard_map(per_device, mesh=mesh, in_specs=in_specs, out_specs=out_specs, check_vma=False)
```

```python
import functools
import math

import jax
import jax.numpy as jnp
from jax import lax
from jax.experimental import pallas as pl
from jax.experimental.pallas import tpu as pltpu
from jax.sharding import PartitionSpec as P

HEAD = 128
BLK = 64
LIST = 16
DOCS = 8
HIDDEN = -1e30
FAR = 1 << 24
EXTRA = 8
CHUNK = 128
CLOSE = 512
RISING = 384
FALLING = 256
NEAR_ROWS = CLOSE + RISING + 2 * FALLING
FAR_ROWS = RISING
LINE = 128
COUNTS = 64
NEAR_SIZES = (2, 4, 6, 8, 10, 12, 16)
FAR_SIZES = (0, 2, 4, 6, 8, 16)


def project_kernel(feat_hbm, gain_hbm, weight_hbm, out, feat, gain, weight, sems):
    tokens = feat.shape[0]
    blocks, _, width = weight.shape
    small = [
        pltpu.make_async_copy(feat_hbm, feat, sems.at[blocks]),
        pltpu.make_async_copy(gain_hbm, gain, sems.at[blocks + 1]),
    ]
    copies = [
        pltpu.make_async_copy(weight_hbm.at[:, pl.ds(j * width, width)], weight.at[j], sems.at[j]) for j in range(blocks)
    ]
    for copy in small + copies:
        copy.start()
    for copy in small:
        copy.wait()
    x = feat[...].astype(jnp.float32)
    g = x * gain[...]
    high = g.astype(jnp.bfloat16)
    both = jnp.concatenate([high, (g - high.astype(jnp.float32)).astype(jnp.bfloat16)], axis=0)
    total = jnp.sum(x * x, axis=1, keepdims=True)
    row = jnp.broadcast_to(total, (tokens, 128)).T[:EXTRA]
    top = row.astype(jnp.bfloat16).astype(jnp.float32)
    which = lax.broadcasted_iota(jnp.int32, (EXTRA, 128), 0)
    tail = jnp.where(which == 0, top, jnp.where(which == 1, row - top, 0.0)).astype(jnp.bfloat16)
    cols = out.shape[2]
    for h in range(out.shape[0]):
        out[h, tokens:, :128] = tail
        out[h, tokens:, 128:] = jnp.zeros_like(tail)
    for j, copy in enumerate(copies):
        copy.wait()
        product = jnp.dot(both, weight[j], preferred_element_type=jnp.float32)
        product = (product[:tokens] + product[tokens:]).astype(jnp.bfloat16)
        for i in range(width // cols):
            out[j * (width // cols) + i, :tokens, :] = product[:, i * cols : (i + 1) * cols]


def project(features, norm_gain, kv_weight, heads):
    tokens, width = features.shape
    cols = kv_weight.shape[1] // heads
    blocks = 4
    anywhere = pl.BlockSpec(memory_space=pl.ANY)
    return pl.pallas_call(
        project_kernel,
        in_specs=[anywhere] * 3,
        out_specs=pl.BlockSpec(memory_space=pltpu.VMEM),
        out_shape=jax.ShapeDtypeStruct((heads, tokens + EXTRA, cols), jnp.bfloat16),
        scratch_shapes=[
            pltpu.VMEM((tokens, width), features.dtype),
            pltpu.VMEM((1, width), norm_gain.dtype),
            pltpu.VMEM((blocks, width, kv_weight.shape[1] // blocks), kv_weight.dtype),
            pltpu.SemaphoreType.DMA((blocks + 2,)),
        ],
        compiler_params=pltpu.CompilerParams(vmem_limit_bytes=60 << 20),
        name="project",
    )(features, norm_gain.reshape(1, width), kv_weight)


def reduce_kernel(width, parts, out, work):
    tokens = out.shape[0]
    total = jnp.sum(parts[:, tokens:, :128].astype(jnp.float32), axis=0)
    squares = jnp.broadcast_to(total[0:1] + total[1:2], (128, tokens)).T
    inverse = lax.rsqrt(squares / width + 1e-05)
    for half in range(2):
        cols = slice(half * 128, half * 128 + 128)
        kept = parts[0, :tokens, cols].astype(jnp.float32)
        for s in range(1, parts.shape[0]):
            kept = kept + parts[s, :tokens, cols].astype(jnp.float32)
        kept = (kept * inverse).astype(jnp.bfloat16)
        out[:, cols] = kept
        work[:, cols] = kept


def prepare_kernel(blocks_dev, place, lists, docs, table, seen):
    t = place[0]
    z = t // 4
    low = lax.rem(t, 4)
    units = lists.shape[0]
    d = docs[...]
    starts = [0] + [jnp.sum((d < doc).astype(jnp.int32)) for doc in range(1, DOCS)]
    for doc in range(DOCS):
        table[units * LINE + doc] = starts[doc]
    for c in range(seen.shape[0]):
        seen[c] = -1

    def unit_lists(u, carry):
        block = t * blocks_dev + lax.rem(u, blocks_dev)
        first = block * BLK
        begin = 0
        for doc in range(1, DOCS):
            begin = jnp.where(starts[doc] <= first, starts[doc], begin)
        least = begin // BLK
        base = u * LINE
        for e in range(LIST):
            table[base + e] = 0
            table[base + LIST + e] = FAR
            table[base + 2 * LIST + e] = 0
            table[base + 3 * LIST + e] = FAR
        near = 0
        far = 0
        for e in range(LIST):
            c = lists[u, e]
            keep = (c >= least) & (seen[c] != u)
            seen[c] = u
            away = z - c // 8
            x = lax.rem(c // 2, 4) ^ low
            inner = lax.rem(c, 2) * BLK
            y = x >> 1
            core = x & 1
            is_near = (away <= 1) | (y == 0) | (away >= 5)
            near_row = jnp.where(
                away <= 1,
                y * (CLOSE // 2) + away * CHUNK,
                jnp.where(away <= 4, CLOSE + (away - 2) * CHUNK, CLOSE + RISING + y * FALLING + (6 - away) * CHUNK),
            )
            near_row += core * NEAR_ROWS + inner
            far_row = core * FAR_ROWS + (away - 2) * CHUNK + inner
            at = base + jnp.where(is_near, near, 2 * LIST + far)
            row = jnp.where(is_near, near_row, far_row)
            table[at] = jnp.where(keep, row, 0)
            table[at + LIST] = jnp.where(keep, c * BLK, FAR)
            near = near + (keep & is_near).astype(jnp.int32)
            far = far + (keep & ~is_near).astype(jnp.int32)
        counts = units * LINE + COUNTS + u
        table[counts] = near
        table[counts + units] = far
        return carry

    lax.fori_loop(0, units, unit_lists, 0)


def scores(blocks, base, block, extra, begins, table, queries, held):
    pieces = [held[pl.ds(pl.multiple_of(table[base + e], BLK), BLK), :] for e in range(blocks)]
    pieces += [rows for rows, _ in extra]
    kv = jnp.concatenate(pieces, axis=0)
    lane = lax.rem(lax.broadcasted_iota(jnp.int32, (1, 128), 1), BLK)
    sub = lax.broadcasted_iota(jnp.int32, (BLK, 128), 0)
    pos_i = block * BLK + lane
    masks = []
    for e in range(blocks):
        pos_j = table[base + LIST + e] + sub
        masks.append((pos_j >= begins) & (pos_j <= pos_i))
    masks += [(sub == lane) & allowed for _, allowed in extra]
    mask = jnp.concatenate(masks, axis=0)
    mask = jnp.concatenate([mask] * (queries.shape[0] // 128), axis=1)
    s = lax.dot_general(kv[:, :HEAD], queries, (((1,), (1,)), ((), ())), preferred_element_type=jnp.float32)
    return jnp.where(mask, s, HIDDEN), kv[:, HEAD:]


def weigh(p, values):
    return lax.dot_general(
        values, p.astype(jnp.bfloat16), (((0,), (0,)), ((), ())), preferred_element_type=jnp.float32
    )


def unit_state(blocks_dev, u, t, table, q):
    steps, heads, tokens, head_dim = q.shape
    units = steps * blocks_dev
    k = u // blocks_dev
    half = lax.rem(u, blocks_dev)
    block = t * blocks_dev + half
    rows = pl.ds(pl.multiple_of(half * BLK, BLK), BLK)
    queries = q[k, :, rows, :].reshape(heads * BLK, head_dim)
    pos_i = block * BLK + lax.rem(lax.broadcasted_iota(jnp.int32, (1, 128), 1), BLK)
    begins = jnp.zeros((1, 128), jnp.int32)
    for doc in range(1, DOCS):
        start = table[units * LINE + doc]
        begins = jnp.where(start <= pos_i, start, begins)
    return k, block, rows, queries, begins


def per_size(sizes, n, run):
    least = -1
    for size in sizes:
        pl.when((n > least) & (n <= size))(functools.partial(run, size))
        least = size


SCALE = math.log2(math.e) / math.sqrt(HEAD)


def hold(held, parts):
    row = 0
    for part in parts:
        held[row : row + part.shape[0]] = part[...]
        row += part.shape[0]


def own_kernel(blocks_dev, q, own, state, sums):
    steps, heads, tokens, head_dim = q.shape

    def body(u, carry):
        k = u // blocks_dev
        rows = pl.ds(pl.multiple_of(lax.rem(u, blocks_dev) * BLK, BLK), BLK)
        queries = q[k, :, rows, :].reshape(heads * BLK, head_dim)
        extra = [(own[m, 0, rows, :], m <= k) for m in range(steps)]
        s, values = scores(0, 0, 0, extra, None, None, queries, None)
        top = jnp.max(s, axis=0, keepdims=True)
        p = jnp.exp2((s - top) * SCALE)
        sums[u, 0:1] = top
        sums[u, 1:2] = jnp.sum(p, axis=0, keepdims=True)
        state[u] = weigh(p, values)
        return carry

    lax.fori_loop(0, steps * blocks_dev, body, 0)


def add_blocks(size, u, base, block, begins, table, queries, held, state, sums):
    top, total, summed = sums[u, 0:1], sums[u, 1:2], state[u]
    if size:
        s, values = scores(size, base, block, [], begins, table, queries, held)
        new_top = jnp.maximum(top, jnp.max(s, axis=0, keepdims=True))
        p = jnp.exp2((s - new_top) * SCALE)
        factor = jnp.exp2((top - new_top) * SCALE)
        total = total * factor + jnp.sum(p, axis=0, keepdims=True)
        summed = summed * factor + weigh(p, values)
        top = new_top
    return top, total, summed


def near_kernel(blocks_dev, place, table, q, old_state, old_sums, mine, theirs, state, sums, held):
    t = place[0]
    units = q.shape[0] * blocks_dev
    hold(held, (mine, theirs))

    def body(u, carry):
        k, block, rows, queries, begins = unit_state(blocks_dev, u, t, table, q)

        def run(size):
            top, total, summed = add_blocks(
                size, u, u * LINE, block, begins, table, queries, held, old_state, old_sums
            )
            sums[u, 0:1] = top
            sums[u, 1:2] = total
            state[u] = summed

        per_size(NEAR_SIZES, table[units * LINE + COUNTS + u], run)
        return carry

    lax.fori_loop(0, units, body, 0)


def far_kernel(blocks_dev, place, table, q, state, sums, mine, theirs, out, held, result, sems):
    t = place[0]
    steps, heads, tokens, head_dim = q.shape
    units = steps * blocks_dev
    hold(held, (mine, theirs))

    def copy(u):
        rows = pl.ds(pl.multiple_of(lax.rem(u, blocks_dev) * BLK, BLK), BLK)
        return pltpu.make_async_copy(result.at[u], out.at[u // blocks_dev, :, rows, :], sems.at[u])

    def body(u, carry):
        k, block, rows, queries, begins = unit_state(blocks_dev, u, t, table, q)

        def run(size):
            top, total, summed = add_blocks(
                size, u, u * LINE + 2 * LIST, block, begins, table, queries, held, state, sums
            )
            result[u] = (summed * (1.0 / total)).T.astype(jnp.bfloat16).reshape(heads, BLK, head_dim)

        per_size(FAR_SIZES, table[units * LINE + COUNTS + units + u], run)
        copy(u).start()
        return carry

    lax.fori_loop(0, units, body, 0)
    lax.fori_loop(0, units, lambda u, c: (copy(u).wait(), c)[1], 0)


SMEM_ALL = pl.BlockSpec(memory_space=pltpu.SMEM)
VMEM_WHOLE = pl.BlockSpec(memory_space=pltpu.VMEM)


def limit(mib):
    return pltpu.CompilerParams(vmem_limit_bytes=mib << 20)


def state_shapes(queries, blocks_dev):
    steps, heads, tokens, head_dim = queries.shape
    units = steps * blocks_dev
    return [
        jax.ShapeDtypeStruct((units, head_dim, heads * BLK), jnp.float32),
        jax.ShapeDtypeStruct((units, 8, heads * BLK), jnp.float32),
    ]


def attend_own(queries, step_kv, blocks_dev):
    return pl.pallas_call(
        functools.partial(own_kernel, blocks_dev),
        in_specs=[VMEM_WHOLE] * 2,
        out_specs=[VMEM_WHOLE] * 2,
        out_shape=state_shapes(queries, blocks_dev),
        compiler_params=limit(16),
        name="attend_own",
    )(queries, step_kv)


def attend_near(place, table, queries, state, sums, mine, theirs, blocks_dev):
    return pl.pallas_call(
        functools.partial(near_kernel, blocks_dev),
        in_specs=[SMEM_ALL] * 2 + [VMEM_WHOLE] * 5,
        out_specs=[VMEM_WHOLE] * 2,
        out_shape=state_shapes(queries, blocks_dev),
        input_output_aliases={3: 0, 4: 1},
        scratch_shapes=[pltpu.VMEM((2 * NEAR_ROWS, mine.shape[1]), jnp.bfloat16)],
        compiler_params=limit(24),
        name="attend_near",
    )(place, table, queries, state, sums, mine, theirs)


def attend_far(place, table, queries, state, sums, mine, theirs, blocks_dev):
    steps, heads, tokens, head_dim = queries.shape
    units = steps * blocks_dev
    return pl.pallas_call(
        functools.partial(far_kernel, blocks_dev),
        in_specs=[SMEM_ALL, SMEM_ALL] + [VMEM_WHOLE] * 5,
        out_specs=pl.BlockSpec(memory_space=pl.ANY),
        out_shape=jax.ShapeDtypeStruct(queries.shape, jnp.bfloat16),
        scratch_shapes=[
            pltpu.VMEM((2 * FAR_ROWS, 2 * head_dim), jnp.bfloat16),
            pltpu.VMEM((units, heads, BLK, head_dim), jnp.bfloat16),
            pltpu.SemaphoreType.DMA((units,)),
        ],
        compiler_params=limit(24),
        name="attend_far",
    )(place, table, queries, state, sums, mine, theirs)


def per_device(features, norm_gain, kv_weight, queries, step_kv, doc_ids, block_lists):
    sections = lax.axis_size("section")
    seqs = lax.axis_size("seq")
    step_total, local_heads, tok_dev, head_dim = queries.shape
    blocks_dev = tok_dev // BLK
    units = step_total * blocks_dev
    place = lax.axis_index("seq").reshape(1).astype(jnp.int32)

    partial = project(features, norm_gain, kv_weight, sections)
    parts = lax.all_to_all(partial, "section", 0, 0, tiled=True)
    lists = lax.dynamic_slice_in_dim(block_lists, place[0] * blocks_dev, blocks_dev, 1).reshape(units, LIST)
    table = pl.pallas_call(
        functools.partial(prepare_kernel, blocks_dev),
        in_specs=[SMEM_ALL, SMEM_ALL, VMEM_WHOLE],
        out_specs=SMEM_ALL,
        out_shape=jax.ShapeDtypeStruct(((units + 1) * LINE,), jnp.int32),
        scratch_shapes=[pltpu.SMEM((block_lists.shape[1],), jnp.int32)],
        compiler_params=limit(4),
        name="prepare",
    )(place, lists, doc_ids.reshape(-1, 128))

    state, sums = attend_own(queries, step_kv, blocks_dev)
    parts, table, state, sums = lax.optimization_barrier((parts, table, state, sums))
    kv_cache, kv = pl.pallas_call(
        functools.partial(reduce_kernel, float(features.shape[1] * sections)),
        out_shape=[jax.ShapeDtypeStruct((tok_dev, 2 * head_dim), jnp.bfloat16)] * 2,
        compiler_params=limit(8),
        name="reduce",
    )(parts)

    every = range(seqs)

    def along_z(x, levels):
        return lax.ppermute(x, "seq", [(i, (i + 4 * levels) % seqs) for i in every])

    def along_y(x):
        return lax.ppermute(x, "seq", [(i, i ^ 2) for i in every])

    def along_core(x):
        return lax.ppermute(x, "seq", [(i, i ^ 1) for i in every])

    def join(*arrays):
        return jnp.concatenate(arrays, axis=0)

    down1 = along_z(kv, -1)
    up1 = along_z(kv, 1)
    high, low = lax.optimization_barrier((join(kv, down1), join(kv, up1)))
    down23 = along_z(high, -2)
    up23 = along_z(low, 2)
    low_y = along_y(low)
    up4 = along_z(high[tok_dev:], -3)
    falling = join(down23, along_y(down23))
    rising = join(up23, up4)
    far = along_y(rising)
    near = join(low, low_y, rising, falling)
    state, sums = attend_near(place, table, queries, state, sums, near, along_core(near), blocks_dev)
    far, state, sums = lax.optimization_barrier((far, state, sums))
    attended = attend_far(place, table, queries, state, sums, far, along_core(far), blocks_dev)
    return attended, kv_cache[None]


def solution(mesh):
    in_specs = (
        P("seq", "section"),
        P("section"),
        P("section", None),
        P(None, "section", "seq", None),
        P(None, "section", "seq", None),
        P(),
        P(),
    )
    out_specs = (P(None, "section", "seq", None), P("section", "seq", None))
    return jax.shard_map(per_device, mesh=mesh, in_specs=in_specs, out_specs=out_specs, check_vma=False)
```

```python
import functools
import math

import jax
import jax.numpy as jnp
from jax import lax
from jax.experimental import pallas as pl
from jax.experimental.pallas import tpu as pltpu
from jax.sharding import PartitionSpec as P

HEAD = 128
BLK = 64
LIST = 16
DOCS = 8
HIDDEN = -1e30
FAR = 1 << 24
EXTRA = 8
CHUNK = 128
CLOSE = 512
RISING = 384
FALLING = 256
NEAR_ROWS = CLOSE + RISING + 2 * FALLING
FAR_ROWS = RISING
LINE = 128
COUNTS = 64
NEAR_SIZES = (2, 4, 6, 8, 10, 12, 16)
FAR_SIZES = (0, 2, 4, 6, 8, 16)


def project_kernel(feat_hbm, gain_hbm, weight_hbm, out, feat, gain, weight, sems):
    tokens = feat.shape[0]
    blocks, _, width = weight.shape
    small = [
        pltpu.make_async_copy(feat_hbm, feat, sems.at[blocks]),
        pltpu.make_async_copy(gain_hbm, gain, sems.at[blocks + 1]),
    ]
    copies = [
        pltpu.make_async_copy(weight_hbm.at[:, pl.ds(j * width, width)], weight.at[j], sems.at[j]) for j in range(blocks)
    ]
    for copy in small + copies:
        copy.start()
    for copy in small:
        copy.wait()
    x = feat[...].astype(jnp.float32)
    g = x * gain[...]
    high = g.astype(jnp.bfloat16)
    both = jnp.concatenate([high, (g - high.astype(jnp.float32)).astype(jnp.bfloat16)], axis=0)
    total = jnp.sum(x * x, axis=1, keepdims=True)
    row = jnp.broadcast_to(total, (tokens, 128)).T[:EXTRA]
    top = row.astype(jnp.bfloat16).astype(jnp.float32)
    which = lax.broadcasted_iota(jnp.int32, (EXTRA, 128), 0)
    tail = jnp.where(which == 0, top, jnp.where(which == 1, row - top, 0.0)).astype(jnp.bfloat16)
    cols = out.shape[2]
    for h in range(out.shape[0]):
        out[h, tokens:, :128] = tail
        out[h, tokens:, 128:] = jnp.zeros_like(tail)
    for j, copy in enumerate(copies):
        copy.wait()
        product = jnp.dot(both, weight[j], preferred_element_type=jnp.float32)
        product = (product[:tokens] + product[tokens:]).astype(jnp.bfloat16)
        for i in range(width // cols):
            out[j * (width // cols) + i, :tokens, :] = product[:, i * cols : (i + 1) * cols]


def project(features, norm_gain, kv_weight, heads):
    tokens, width = features.shape
    cols = kv_weight.shape[1] // heads
    blocks = 4
    anywhere = pl.BlockSpec(memory_space=pl.ANY)
    return pl.pallas_call(
        project_kernel,
        in_specs=[anywhere] * 3,
        out_specs=pl.BlockSpec(memory_space=pltpu.VMEM),
        out_shape=jax.ShapeDtypeStruct((heads, tokens + EXTRA, cols), jnp.bfloat16),
        scratch_shapes=[
            pltpu.VMEM((tokens, width), features.dtype),
            pltpu.VMEM((1, width), norm_gain.dtype),
            pltpu.VMEM((blocks, width, kv_weight.shape[1] // blocks), kv_weight.dtype),
            pltpu.SemaphoreType.DMA((blocks + 2,)),
        ],
        compiler_params=pltpu.CompilerParams(vmem_limit_bytes=60 << 20),
        name="project",
    )(features, norm_gain.reshape(1, width), kv_weight)


def reduce_kernel(width, parts, out, work):
    tokens = out.shape[0]
    total = jnp.sum(parts[:, tokens:, :128].astype(jnp.float32), axis=0)
    squares = jnp.broadcast_to(total[0:1] + total[1:2], (128, tokens)).T
    inverse = lax.rsqrt(squares / width + 1e-05)
    for half in range(2):
        cols = slice(half * 128, half * 128 + 128)
        kept = parts[0, :tokens, cols].astype(jnp.float32)
        for s in range(1, parts.shape[0]):
            kept = kept + parts[s, :tokens, cols].astype(jnp.float32)
        kept = (kept * inverse).astype(jnp.bfloat16)
        out[:, cols] = kept
        work[:, cols] = kept


def prepare_kernel(blocks_dev, place, lists, docs, table, seen):
    t = place[0]
    z = t // 4
    low = lax.rem(t, 4)
    units = lists.shape[0]
    d = docs[...]
    starts = [0] + [jnp.sum((d < doc).astype(jnp.int32)) for doc in range(1, DOCS)]
    for doc in range(DOCS):
        table[units * LINE + doc] = starts[doc]
    for c in range(seen.shape[0]):
        seen[c] = -1

    def unit_lists(u, carry):
        block = t * blocks_dev + lax.rem(u, blocks_dev)
        first = block * BLK
        begin = 0
        for doc in range(1, DOCS):
            begin = jnp.where(starts[doc] <= first, starts[doc], begin)
        least = begin // BLK
        base = u * LINE
        for e in range(LIST):
            table[base + e] = 0
            table[base + LIST + e] = FAR
            table[base + 2 * LIST + e] = 0
            table[base + 3 * LIST + e] = FAR
        near = 0
        far = 0
        for e in range(LIST):
            c = lists[u, e]
            keep = (c >= least) & (seen[c] != u)
            seen[c] = u
            away = z - c // 8
            x = lax.rem(c // 2, 4) ^ low
            inner = lax.rem(c, 2) * BLK
            y = x >> 1
            core = x & 1
            is_near = (away <= 1) | (y == 0) | (away >= 5)
            near_row = jnp.where(
                away <= 1,
                y * (CLOSE // 2) + away * CHUNK,
                jnp.where(away <= 4, CLOSE + (away - 2) * CHUNK, CLOSE + RISING + y * FALLING + (6 - away) * CHUNK),
            )
            near_row += core * NEAR_ROWS + inner
            far_row = core * FAR_ROWS + (away - 2) * CHUNK + inner
            at = base + jnp.where(is_near, near, 2 * LIST + far)
            row = jnp.where(is_near, near_row, far_row)
            table[at] = jnp.where(keep, row, 0)
            table[at + LIST] = jnp.where(keep, c * BLK, FAR)
            near = near + (keep & is_near).astype(jnp.int32)
            far = far + (keep & ~is_near).astype(jnp.int32)
        counts = units * LINE + COUNTS + u
        table[counts] = near
        table[counts + units] = far
        return carry

    lax.fori_loop(0, units, unit_lists, 0)


def scores(blocks, base, block, extra, begins, table, queries, held):
    pieces = [held[pl.ds(pl.multiple_of(table[base + e], BLK), BLK), :] for e in range(blocks)]
    pieces += [rows for rows, _ in extra]
    kv = jnp.concatenate(pieces, axis=0)
    lane = lax.rem(lax.broadcasted_iota(jnp.int32, (1, 128), 1), BLK)
    sub = lax.broadcasted_iota(jnp.int32, (BLK, 128), 0)
    pos_i = block * BLK + lane
    masks = []
    for e in range(blocks):
        pos_j = table[base + LIST + e] + sub
        masks.append((pos_j >= begins) & (pos_j <= pos_i))
    masks += [(sub == lane) & allowed for _, allowed in extra]
    mask = jnp.concatenate(masks, axis=0)
    mask = jnp.concatenate([mask] * (queries.shape[0] // 128), axis=1)
    s = lax.dot_general(kv[:, :HEAD], queries, (((1,), (1,)), ((), ())), preferred_element_type=jnp.float32)
    return jnp.where(mask, s, HIDDEN), kv[:, HEAD:]


def weigh(p, values):
    return lax.dot_general(
        values, p.astype(jnp.bfloat16), (((0,), (0,)), ((), ())), preferred_element_type=jnp.float32
    )


def unit_state(blocks_dev, u, t, table, q):
    steps, heads, tokens, head_dim = q.shape
    units = steps * blocks_dev
    k = u // blocks_dev
    half = lax.rem(u, blocks_dev)
    block = t * blocks_dev + half
    rows = pl.ds(pl.multiple_of(half * BLK, BLK), BLK)
    queries = q[k, :, rows, :].reshape(heads * BLK, head_dim)
    pos_i = block * BLK + lax.rem(lax.broadcasted_iota(jnp.int32, (1, 128), 1), BLK)
    begins = jnp.zeros((1, 128), jnp.int32)
    for doc in range(1, DOCS):
        start = table[units * LINE + doc]
        begins = jnp.where(start <= pos_i, start, begins)
    return k, block, rows, queries, begins


def per_size(sizes, n, run):
    least = -1
    for size in sizes:
        pl.when((n > least) & (n <= size))(functools.partial(run, size))
        least = size


SCALE = math.log2(math.e) / math.sqrt(HEAD)


def hold(held, parts):
    row = 0
    for part in parts:
        held[row : row + part.shape[0]] = part[...]
        row += part.shape[0]


def own_kernel(blocks_dev, q, own, state, sums):
    steps, heads, tokens, head_dim = q.shape

    def body(u, carry):
        k = u // blocks_dev
        rows = pl.ds(pl.multiple_of(lax.rem(u, blocks_dev) * BLK, BLK), BLK)
        queries = q[k, :, rows, :].reshape(heads * BLK, head_dim)
        extra = [(own[m, 0, rows, :], m <= k) for m in range(steps)]
        s, values = scores(0, 0, 0, extra, None, None, queries, None)
        top = jnp.max(s, axis=0, keepdims=True)
        p = jnp.exp2((s - top) * SCALE)
        sums[u, 0:1] = top
        sums[u, 1:2] = jnp.sum(p, axis=0, keepdims=True)
        state[u] = weigh(p, values)
        return carry

    lax.fori_loop(0, steps * blocks_dev, body, 0)


def add_blocks(size, u, base, block, begins, table, queries, held, state, sums):
    top, total, summed = sums[u, 0:1], sums[u, 1:2], state[u]
    if size:
        s, values = scores(size, base, block, [], begins, table, queries, held)
        new_top = jnp.maximum(top, jnp.max(s, axis=0, keepdims=True))
        p = jnp.exp2((s - new_top) * SCALE)
        factor = jnp.exp2((top - new_top) * SCALE)
        total = total * factor + jnp.sum(p, axis=0, keepdims=True)
        summed = summed * factor + weigh(p, values)
        top = new_top
    return top, total, summed


def near_kernel(blocks_dev, place, table, q, old_state, old_sums, mine, theirs, state, sums, held):
    t = place[0]
    units = q.shape[0] * blocks_dev
    hold(held, (mine, theirs))

    def body(u, carry):
        k, block, rows, queries, begins = unit_state(blocks_dev, u, t, table, q)

        def run(size):
            top, total, summed = add_blocks(
                size, u, u * LINE, block, begins, table, queries, held, old_state, old_sums
            )
            sums[u, 0:1] = top
            sums[u, 1:2] = total
            state[u] = summed

        per_size(NEAR_SIZES, table[units * LINE + COUNTS + u], run)
        return carry

    lax.fori_loop(0, units, body, 0)


def far_kernel(blocks_dev, place, table, q, state, sums, mine, theirs, out, held, result, sems):
    t = place[0]
    steps, heads, tokens, head_dim = q.shape
    units = steps * blocks_dev
    hold(held, (mine, theirs))

    def copy(u):
        rows = pl.ds(pl.multiple_of(lax.rem(u, blocks_dev) * BLK, BLK), BLK)
        return pltpu.make_async_copy(result.at[u], out.at[u // blocks_dev, :, rows, :], sems.at[u])

    def body(u, carry):
        k, block, rows, queries, begins = unit_state(blocks_dev, u, t, table, q)

        def run(size):
            top, total, summed = add_blocks(
                size, u, u * LINE + 2 * LIST, block, begins, table, queries, held, state, sums
            )
            result[u] = (summed * (1.0 / total)).T.astype(jnp.bfloat16).reshape(heads, BLK, head_dim)

        per_size(FAR_SIZES, table[units * LINE + COUNTS + units + u], run)
        copy(u).start()
        return carry

    lax.fori_loop(0, units, body, 0)
    lax.fori_loop(0, units, lambda u, c: (copy(u).wait(), c)[1], 0)


SMEM_ALL = pl.BlockSpec(memory_space=pltpu.SMEM)
VMEM_WHOLE = pl.BlockSpec(memory_space=pltpu.VMEM)


def limit(mib):
    return pltpu.CompilerParams(vmem_limit_bytes=mib << 20)


def state_shapes(queries, blocks_dev):
    steps, heads, tokens, head_dim = queries.shape
    units = steps * blocks_dev
    return [
        jax.ShapeDtypeStruct((units, head_dim, heads * BLK), jnp.float32),
        jax.ShapeDtypeStruct((units, 8, heads * BLK), jnp.float32),
    ]


def attend_own(queries, step_kv, blocks_dev):
    return pl.pallas_call(
        functools.partial(own_kernel, blocks_dev),
        in_specs=[VMEM_WHOLE] * 2,
        out_specs=[VMEM_WHOLE] * 2,
        out_shape=state_shapes(queries, blocks_dev),
        compiler_params=limit(16),
        name="attend_own",
    )(queries, step_kv)


def attend_near(place, table, queries, state, sums, mine, theirs, blocks_dev):
    return pl.pallas_call(
        functools.partial(near_kernel, blocks_dev),
        in_specs=[SMEM_ALL] * 2 + [VMEM_WHOLE] * 5,
        out_specs=[VMEM_WHOLE] * 2,
        out_shape=state_shapes(queries, blocks_dev),
        input_output_aliases={3: 0, 4: 1},
        scratch_shapes=[pltpu.VMEM((2 * NEAR_ROWS, mine.shape[1]), jnp.bfloat16)],
        compiler_params=limit(24),
        name="attend_near",
    )(place, table, queries, state, sums, mine, theirs)


def attend_far(place, table, queries, state, sums, mine, theirs, blocks_dev):
    steps, heads, tokens, head_dim = queries.shape
    units = steps * blocks_dev
    return pl.pallas_call(
        functools.partial(far_kernel, blocks_dev),
        in_specs=[SMEM_ALL, SMEM_ALL] + [VMEM_WHOLE] * 5,
        out_specs=pl.BlockSpec(memory_space=pl.ANY),
        out_shape=jax.ShapeDtypeStruct(queries.shape, jnp.bfloat16),
        scratch_shapes=[
            pltpu.VMEM((2 * FAR_ROWS, 2 * head_dim), jnp.bfloat16),
            pltpu.VMEM((units, heads, BLK, head_dim), jnp.bfloat16),
            pltpu.SemaphoreType.DMA((units,)),
        ],
        compiler_params=limit(24),
        name="attend_far",
    )(place, table, queries, state, sums, mine, theirs)


def per_device(features, norm_gain, kv_weight, queries, step_kv, doc_ids, block_lists):
    sections = lax.axis_size("section")
    seqs = lax.axis_size("seq")
    step_total, local_heads, tok_dev, head_dim = queries.shape
    blocks_dev = tok_dev // BLK
    units = step_total * blocks_dev
    place = lax.axis_index("seq").reshape(1).astype(jnp.int32)

    partial = project(features, norm_gain, kv_weight, sections)
    parts = lax.all_to_all(partial, "section", 0, 0, tiled=True)
    lists = lax.dynamic_slice_in_dim(block_lists, place[0] * blocks_dev, blocks_dev, 1).reshape(units, LIST)
    table = pl.pallas_call(
        functools.partial(prepare_kernel, blocks_dev),
        in_specs=[SMEM_ALL, SMEM_ALL, VMEM_WHOLE],
        out_specs=SMEM_ALL,
        out_shape=jax.ShapeDtypeStruct(((units + 1) * LINE,), jnp.int32),
        scratch_shapes=[pltpu.SMEM((block_lists.shape[1],), jnp.int32)],
        compiler_params=limit(4),
        name="prepare",
    )(place, lists, doc_ids.reshape(-1, 128))

    state, sums = attend_own(queries, step_kv, blocks_dev)
    parts, table, state, sums = lax.optimization_barrier((parts, table, state, sums))
    kv_cache, kv = pl.pallas_call(
        functools.partial(reduce_kernel, float(features.shape[1] * sections)),
        out_shape=[jax.ShapeDtypeStruct((tok_dev, 2 * head_dim), jnp.bfloat16)] * 2,
        compiler_params=limit(8),
        name="reduce",
    )(parts)

    every = range(seqs)

    levels = range(seqs // 4)

    def along_z(x, moves):
        pairs = [(4 * source + i, 4 * goal + i) for source, goal in moves for i in range(4)]
        return lax.ppermute(x, "seq", sorted(pairs))

    def along_y(x):
        return lax.ppermute(x, "seq", [(i, i ^ 2) for i in every])

    def along_core(x):
        return lax.ppermute(x, "seq", [(i, i ^ 1) for i in every])

    def join(*arrays):
        return jnp.concatenate(arrays, axis=0)

    down1 = along_z(kv, [(3, 2), (2, 1), (1, 0), (0, 7)])
    up1 = along_z(kv, [(z, z + 1) for z in levels[:-1]])
    high, low = lax.optimization_barrier((join(kv, down1), join(kv, up1)))
    down23 = along_z(high, [(1, 7), (0, 6), (7, 5)])
    up23 = along_z(low, [(z, z + 2) for z in levels[:-2]])
    low_y = along_y(low)
    up4 = along_z(high[tok_dev:], [(7, 4), (0, 5), (1, 6), (2, 7)])
    falling = join(down23, along_y(down23))
    rising = join(up23, up4)
    far = along_y(rising)
    near = join(low, low_y, rising, falling)
    state, sums = attend_near(place, table, queries, state, sums, near, along_core(near), blocks_dev)
    far, state, sums = lax.optimization_barrier((far, state, sums))
    attended = attend_far(place, table, queries, state, sums, far, along_core(far), blocks_dev)
    return attended, kv_cache[None]


def solution(mesh):
    in_specs = (
        P("seq", "section"),
        P("section"),
        P("section", None),
        P(None, "section", "seq", None),
        P(None, "section", "seq", None),
        P(),
        P(),
    )
    out_specs = (P(None, "section", "seq", None), P("section", "seq", None))
    return jax.shard_map(per_device, mesh=mesh, in_specs=in_specs, out_specs=out_specs, check_vma=False)
```

```python
import functools
import math

import jax
import jax.numpy as jnp
from jax import lax
from jax.experimental import pallas as pl
from jax.experimental.pallas import tpu as pltpu
from jax.sharding import PartitionSpec as P

HEAD = 128
BLK = 64
LIST = 16
DOCS = 8
HIDDEN = -1e30
FAR = 1 << 24
EXTRA = 8
CHUNK = 128
CLOSE = 512
RISING = 384
FALLING = 256
NEAR_ROWS = CLOSE + RISING + 2 * FALLING
FAR_ROWS = RISING
LINE = 128
COUNTS = 64
NEAR_SIZES = (2, 4, 6, 8, 10, 12, 16)
FAR_SIZES = (0, 2, 4, 6, 8, 16)


def project_kernel(feat_hbm, gain_hbm, weight_hbm, out, feat, gain, weight, sems):
    tokens = feat.shape[0]
    blocks, _, width = weight.shape
    small = [
        pltpu.make_async_copy(feat_hbm, feat, sems.at[blocks]),
        pltpu.make_async_copy(gain_hbm, gain, sems.at[blocks + 1]),
    ]
    copies = [
        pltpu.make_async_copy(weight_hbm.at[:, pl.ds(j * width, width)], weight.at[j], sems.at[j]) for j in range(blocks)
    ]
    for copy in small + copies:
        copy.start()
    for copy in small:
        copy.wait()
    x = feat[...].astype(jnp.float32)
    g = x * gain[...]
    high = g.astype(jnp.bfloat16)
    both = jnp.concatenate([high, (g - high.astype(jnp.float32)).astype(jnp.bfloat16)], axis=0)
    total = jnp.sum(x * x, axis=1, keepdims=True)
    row = jnp.broadcast_to(total, (tokens, 128)).T[:EXTRA]
    top = row.astype(jnp.bfloat16).astype(jnp.float32)
    which = lax.broadcasted_iota(jnp.int32, (EXTRA, 128), 0)
    tail = jnp.where(which == 0, top, jnp.where(which == 1, row - top, 0.0)).astype(jnp.bfloat16)
    cols = out.shape[2]
    for h in range(out.shape[0]):
        out[h, tokens:, :128] = tail
        out[h, tokens:, 128:] = jnp.zeros_like(tail)
    for j, copy in enumerate(copies):
        copy.wait()
        product = jnp.dot(both, weight[j], preferred_element_type=jnp.float32)
        product = (product[:tokens] + product[tokens:]).astype(jnp.bfloat16)
        for i in range(width // cols):
            out[j * (width // cols) + i, :tokens, :] = product[:, i * cols : (i + 1) * cols]


def project(features, norm_gain, kv_weight, heads):
    tokens, width = features.shape
    cols = kv_weight.shape[1] // heads
    blocks = 4
    anywhere = pl.BlockSpec(memory_space=pl.ANY)
    return pl.pallas_call(
        project_kernel,
        in_specs=[anywhere] * 3,
        out_specs=pl.BlockSpec(memory_space=pltpu.VMEM),
        out_shape=jax.ShapeDtypeStruct((heads, tokens + EXTRA, cols), jnp.bfloat16),
        scratch_shapes=[
            pltpu.VMEM((tokens, width), features.dtype),
            pltpu.VMEM((1, width), norm_gain.dtype),
            pltpu.VMEM((blocks, width, kv_weight.shape[1] // blocks), kv_weight.dtype),
            pltpu.SemaphoreType.DMA((blocks + 2,)),
        ],
        compiler_params=pltpu.CompilerParams(vmem_limit_bytes=60 << 20),
        name="project",
    )(features, norm_gain.reshape(1, width), kv_weight)


def reduce_kernel(width, parts, out, work):
    tokens = out.shape[0]
    total = jnp.sum(parts[:, tokens:, :128].astype(jnp.float32), axis=0)
    squares = jnp.broadcast_to(total[0:1] + total[1:2], (128, tokens)).T
    inverse = lax.rsqrt(squares / width + 1e-05)
    for half in range(2):
        cols = slice(half * 128, half * 128 + 128)
        kept = parts[0, :tokens, cols].astype(jnp.float32)
        for s in range(1, parts.shape[0]):
            kept = kept + parts[s, :tokens, cols].astype(jnp.float32)
        kept = (kept * inverse).astype(jnp.bfloat16)
        out[:, cols] = kept
        work[:, cols] = kept


def prepare_kernel(blocks_dev, place, lists, docs, table, seen):
    t = place[0]
    z = t // 4
    low = lax.rem(t, 4)
    units = lists.shape[0]
    d = docs[...]
    starts = [0] + [jnp.sum((d < doc).astype(jnp.int32)) for doc in range(1, DOCS)]
    for doc in range(DOCS):
        table[units * LINE + doc] = starts[doc]
    for c in range(seen.shape[0]):
        seen[c] = -1

    def unit_lists(u, carry):
        block = t * blocks_dev + lax.rem(u, blocks_dev)
        first = block * BLK
        begin = 0
        for doc in range(1, DOCS):
            begin = jnp.where(starts[doc] <= first, starts[doc], begin)
        least = begin // BLK
        base = u * LINE
        for e in range(LIST):
            table[base + e] = 0
            table[base + LIST + e] = FAR
            table[base + 2 * LIST + e] = 0
            table[base + 3 * LIST + e] = FAR
        near = 0
        far = 0
        for e in range(LIST):
            c = lists[u, e]
            keep = (c >= least) & (seen[c] != u)
            seen[c] = u
            away = z - c // 8
            x = lax.rem(c // 2, 4) ^ low
            inner = lax.rem(c, 2) * BLK
            y = x >> 1
            core = x & 1
            is_near = (away <= 1) | (y == 0) | (away >= 5)
            near_row = jnp.where(
                away <= 1,
                y * (CLOSE // 2) + away * CHUNK,
                jnp.where(away <= 4, CLOSE + (away - 2) * CHUNK, CLOSE + RISING + y * FALLING + (6 - away) * CHUNK),
            )
            near_row += core * NEAR_ROWS + inner
            far_row = core * FAR_ROWS + (away - 2) * CHUNK + inner
            at = base + jnp.where(is_near, near, 2 * LIST + far)
            row = jnp.where(is_near, near_row, far_row)
            table[at] = jnp.where(keep, row, 0)
            table[at + LIST] = jnp.where(keep, c * BLK, FAR)
            near = near + (keep & is_near).astype(jnp.int32)
            far = far + (keep & ~is_near).astype(jnp.int32)
        counts = units * LINE + COUNTS + u
        table[counts] = near
        table[counts + units] = far
        return carry

    lax.fori_loop(0, units, unit_lists, 0)


def scores(blocks, base, block, extra, begins, table, queries, held):
    pieces = [held[pl.ds(pl.multiple_of(table[base + e], BLK), BLK), :] for e in range(blocks)]
    pieces += [rows for rows, _ in extra]
    kv = jnp.concatenate(pieces, axis=0)
    lane = lax.rem(lax.broadcasted_iota(jnp.int32, (1, 128), 1), BLK)
    sub = lax.broadcasted_iota(jnp.int32, (BLK, 128), 0)
    pos_i = block * BLK + lane
    masks = []
    for e in range(blocks):
        pos_j = table[base + LIST + e] + sub
        masks.append((pos_j >= begins) & (pos_j <= pos_i))
    masks += [(sub == lane) & allowed for _, allowed in extra]
    mask = jnp.concatenate(masks, axis=0)
    mask = jnp.concatenate([mask] * (queries.shape[0] // 128), axis=1)
    s = lax.dot_general(kv[:, :HEAD], queries, (((1,), (1,)), ((), ())), preferred_element_type=jnp.float32)
    return jnp.where(mask, s, HIDDEN), kv[:, HEAD:]


def weigh(p, values):
    return lax.dot_general(
        values, p.astype(jnp.bfloat16), (((0,), (0,)), ((), ())), preferred_element_type=jnp.float32
    )


def unit_state(blocks_dev, u, t, table, q):
    steps, heads, tokens, head_dim = q.shape
    units = steps * blocks_dev
    k = u // blocks_dev
    half = lax.rem(u, blocks_dev)
    block = t * blocks_dev + half
    rows = pl.ds(pl.multiple_of(half * BLK, BLK), BLK)
    queries = q[k, :, rows, :].reshape(heads * BLK, head_dim)
    pos_i = block * BLK + lax.rem(lax.broadcasted_iota(jnp.int32, (1, 128), 1), BLK)
    begins = jnp.zeros((1, 128), jnp.int32)
    for doc in range(1, DOCS):
        start = table[units * LINE + doc]
        begins = jnp.where(start <= pos_i, start, begins)
    return k, block, rows, queries, begins


def per_size(sizes, n, run):
    least = -1
    for size in sizes:
        pl.when((n > least) & (n <= size))(functools.partial(run, size))
        least = size


SCALE = math.log2(math.e) / math.sqrt(HEAD)


def hold(held, parts):
    row = 0
    for part in parts:
        held[row : row + part.shape[0]] = part[...]
        row += part.shape[0]


def own_kernel(blocks_dev, q, own, state, sums):
    steps, heads, tokens, head_dim = q.shape

    def body(u, carry):
        k = u // blocks_dev
        rows = pl.ds(pl.multiple_of(lax.rem(u, blocks_dev) * BLK, BLK), BLK)
        queries = q[k, :, rows, :].reshape(heads * BLK, head_dim)
        extra = [(own[m, 0, rows, :], m <= k) for m in range(steps)]
        s, values = scores(0, 0, 0, extra, None, None, queries, None)
        top = jnp.max(s, axis=0, keepdims=True)
        p = jnp.exp2((s - top) * SCALE)
        sums[u, 0:1] = top
        sums[u, 1:2] = jnp.sum(p, axis=0, keepdims=True)
        state[u] = weigh(p, values)
        return carry

    lax.fori_loop(0, steps * blocks_dev, body, 0)


def add_blocks(size, u, base, block, begins, table, queries, held, state, sums):
    top, total, summed = sums[u, 0:1], sums[u, 1:2], state[u]
    if size:
        s, values = scores(size, base, block, [], begins, table, queries, held)
        new_top = jnp.maximum(top, jnp.max(s, axis=0, keepdims=True))
        p = jnp.exp2((s - new_top) * SCALE)
        factor = jnp.exp2((top - new_top) * SCALE)
        total = total * factor + jnp.sum(p, axis=0, keepdims=True)
        summed = summed * factor + weigh(p, values)
        top = new_top
    return top, total, summed


def near_kernel(blocks_dev, place, table, q, old_state, old_sums, mine, theirs, state, sums, held):
    t = place[0]
    units = q.shape[0] * blocks_dev
    hold(held, (mine, theirs))

    def body(u, carry):
        k, block, rows, queries, begins = unit_state(blocks_dev, u, t, table, q)

        def run(size):
            top, total, summed = add_blocks(
                size, u, u * LINE, block, begins, table, queries, held, old_state, old_sums
            )
            sums[u, 0:1] = top
            sums[u, 1:2] = total
            state[u] = summed

        per_size(NEAR_SIZES, table[units * LINE + COUNTS + u], run)
        return carry

    lax.fori_loop(0, units, body, 0)


def far_kernel(blocks_dev, place, table, q, state, sums, mine, theirs, out, held, result, sems):
    t = place[0]
    steps, heads, tokens, head_dim = q.shape
    units = steps * blocks_dev
    hold(held, (mine, theirs))

    def copy(u):
        rows = pl.ds(pl.multiple_of(lax.rem(u, blocks_dev) * BLK, BLK), BLK)
        return pltpu.make_async_copy(result.at[u], out.at[u // blocks_dev, :, rows, :], sems.at[u])

    def body(u, carry):
        k, block, rows, queries, begins = unit_state(blocks_dev, u, t, table, q)

        def run(size):
            top, total, summed = add_blocks(
                size, u, u * LINE + 2 * LIST, block, begins, table, queries, held, state, sums
            )
            result[u] = (summed * (1.0 / total)).T.astype(jnp.bfloat16).reshape(heads, BLK, head_dim)

        per_size(FAR_SIZES, table[units * LINE + COUNTS + units + u], run)
        copy(u).start()
        return carry

    lax.fori_loop(0, units, body, 0)
    lax.fori_loop(0, units, lambda u, c: (copy(u).wait(), c)[1], 0)


SMEM_ALL = pl.BlockSpec(memory_space=pltpu.SMEM)
VMEM_WHOLE = pl.BlockSpec(memory_space=pltpu.VMEM)


def limit(mib):
    return pltpu.CompilerParams(vmem_limit_bytes=mib << 20)


def state_shapes(queries, blocks_dev):
    steps, heads, tokens, head_dim = queries.shape
    units = steps * blocks_dev
    return [
        jax.ShapeDtypeStruct((units, head_dim, heads * BLK), jnp.float32),
        jax.ShapeDtypeStruct((units, 8, heads * BLK), jnp.float32),
    ]


def attend_own(queries, step_kv, blocks_dev):
    return pl.pallas_call(
        functools.partial(own_kernel, blocks_dev),
        in_specs=[VMEM_WHOLE] * 2,
        out_specs=[VMEM_WHOLE] * 2,
        out_shape=state_shapes(queries, blocks_dev),
        compiler_params=limit(16),
        name="attend_own",
    )(queries, step_kv)


def attend_near(place, table, queries, state, sums, mine, theirs, blocks_dev):
    return pl.pallas_call(
        functools.partial(near_kernel, blocks_dev),
        in_specs=[SMEM_ALL] * 2 + [VMEM_WHOLE] * 5,
        out_specs=[VMEM_WHOLE] * 2,
        out_shape=state_shapes(queries, blocks_dev),
        input_output_aliases={3: 0, 4: 1},
        scratch_shapes=[pltpu.VMEM((2 * NEAR_ROWS, mine.shape[1]), jnp.bfloat16)],
        compiler_params=limit(24),
        name="attend_near",
    )(place, table, queries, state, sums, mine, theirs)


def attend_far(place, table, queries, state, sums, mine, theirs, blocks_dev):
    steps, heads, tokens, head_dim = queries.shape
    units = steps * blocks_dev
    return pl.pallas_call(
        functools.partial(far_kernel, blocks_dev),
        in_specs=[SMEM_ALL, SMEM_ALL] + [VMEM_WHOLE] * 5,
        out_specs=pl.BlockSpec(memory_space=pl.ANY),
        out_shape=jax.ShapeDtypeStruct(queries.shape, jnp.bfloat16),
        scratch_shapes=[
            pltpu.VMEM((2 * FAR_ROWS, 2 * head_dim), jnp.bfloat16),
            pltpu.VMEM((units, heads, BLK, head_dim), jnp.bfloat16),
            pltpu.SemaphoreType.DMA((units,)),
        ],
        compiler_params=limit(24),
        name="attend_far",
    )(place, table, queries, state, sums, mine, theirs)


def per_device(features, norm_gain, kv_weight, queries, step_kv, doc_ids, block_lists):
    sections = lax.axis_size("section")
    seqs = lax.axis_size("seq")
    step_total, local_heads, tok_dev, head_dim = queries.shape
    blocks_dev = tok_dev // BLK
    units = step_total * blocks_dev
    place = lax.axis_index("seq").reshape(1).astype(jnp.int32)

    partial = project(features, norm_gain, kv_weight, sections)
    parts = lax.all_to_all(partial, "section", 0, 0, tiled=True)
    lists = lax.dynamic_slice_in_dim(block_lists, place[0] * blocks_dev, blocks_dev, 1).reshape(units, LIST)
    table = pl.pallas_call(
        functools.partial(prepare_kernel, blocks_dev),
        in_specs=[SMEM_ALL, SMEM_ALL, VMEM_WHOLE],
        out_specs=SMEM_ALL,
        out_shape=jax.ShapeDtypeStruct(((units + 1) * LINE,), jnp.int32),
        scratch_shapes=[pltpu.SMEM((block_lists.shape[1],), jnp.int32)],
        compiler_params=limit(4),
        name="prepare",
    )(place, lists, doc_ids.reshape(-1, 128))

    state, sums = attend_own(queries, step_kv, blocks_dev)
    parts, table, state, sums = lax.optimization_barrier((parts, table, state, sums))
    kv_cache, kv = pl.pallas_call(
        functools.partial(reduce_kernel, float(features.shape[1] * sections)),
        out_shape=[jax.ShapeDtypeStruct((tok_dev, 2 * head_dim), jnp.bfloat16)] * 2,
        compiler_params=limit(8),
        name="reduce",
    )(parts)

    every = range(seqs)

    def along_z(x, levels):
        return lax.ppermute(x, "seq", [(i, (i + 4 * levels) % seqs) for i in every])

    def along_y(x):
        return lax.ppermute(x, "seq", [(i, i ^ 2) for i in every])

    def along_core(x):
        return lax.ppermute(x, "seq", [(i, i ^ 1) for i in every])

    def join(*arrays):
        return jnp.concatenate(arrays, axis=0)

    moves = [(4 * z + i, (4 * z - 4) % seqs + i) for z in range(4) for i in range(4)]
    down1 = lax.ppermute(kv, "seq", moves)
    up1 = along_z(kv, 1)
    high, low = lax.optimization_barrier((join(kv, down1), join(kv, up1)))
    down23 = along_z(high, -2)
    up23 = along_z(low, 2)
    low_y = along_y(low)
    up4 = along_z(high[tok_dev:], -3)
    falling = join(down23, along_y(down23))
    rising = join(up23, up4)
    far = along_y(rising)
    near = join(low, low_y, rising, falling)
    state, sums = attend_near(place, table, queries, state, sums, near, along_core(near), blocks_dev)
    far, state, sums = lax.optimization_barrier((far, state, sums))
    attended = attend_far(place, table, queries, state, sums, far, along_core(far), blocks_dev)
    return attended, kv_cache[None]


def solution(mesh):
    in_specs = (
        P("seq", "section"),
        P("section"),
        P("section", None),
        P(None, "section", "seq", None),
        P(None, "section", "seq", None),
        P(),
        P(),
    )
    out_specs = (P(None, "section", "seq", None), P("section", "seq", None))
    return jax.shard_map(per_device, mesh=mesh, in_specs=in_specs, out_specs=out_specs, check_vma=False)
```

```python
import functools
import math

import jax
import jax.numpy as jnp
from jax import lax
from jax.experimental import pallas as pl
from jax.experimental.pallas import tpu as pltpu
from jax.sharding import PartitionSpec as P

HEAD = 128
BLK = 64
LIST = 16
DOCS = 8
HIDDEN = -1e30
FAR = 1 << 24
EXTRA = 8
CHUNK = 128
CLOSE = 512
RISING = 384
FALLING = 256
NEAR_ROWS = CLOSE + RISING + 2 * FALLING
FAR_ROWS = RISING
LINE = 128
COUNTS = 64
NEAR_SIZES = (2, 4, 6, 8, 10, 12, 16)
FAR_SIZES = (0, 2, 4, 6, 8, 16)


def project_kernel(feat_hbm, gain_hbm, weight_hbm, out, feat, gain, weight, sems):
    tokens = feat.shape[0]
    blocks, _, width = weight.shape
    small = [
        pltpu.make_async_copy(feat_hbm, feat, sems.at[blocks]),
        pltpu.make_async_copy(gain_hbm, gain, sems.at[blocks + 1]),
    ]
    copies = [
        pltpu.make_async_copy(weight_hbm.at[:, pl.ds(j * width, width)], weight.at[j], sems.at[j]) for j in range(blocks)
    ]
    for copy in small + copies:
        copy.start()
    for copy in small:
        copy.wait()
    x = feat[...].astype(jnp.float32)
    g = x * gain[...]
    high = g.astype(jnp.bfloat16)
    both = jnp.concatenate([high, (g - high.astype(jnp.float32)).astype(jnp.bfloat16)], axis=0)
    total = jnp.sum(x * x, axis=1, keepdims=True)
    row = jnp.broadcast_to(total, (tokens, 128)).T[:EXTRA]
    top = row.astype(jnp.bfloat16).astype(jnp.float32)
    which = lax.broadcasted_iota(jnp.int32, (EXTRA, 128), 0)
    tail = jnp.where(which == 0, top, jnp.where(which == 1, row - top, 0.0)).astype(jnp.bfloat16)
    cols = out.shape[2]
    for h in range(out.shape[0]):
        out[h, tokens:, :128] = tail
        out[h, tokens:, 128:] = jnp.zeros_like(tail)
    for j, copy in enumerate(copies):
        copy.wait()
        product = jnp.dot(both, weight[j], preferred_element_type=jnp.float32)
        product = (product[:tokens] + product[tokens:]).astype(jnp.bfloat16)
        for i in range(width // cols):
            out[j * (width // cols) + i, :tokens, :] = product[:, i * cols : (i + 1) * cols]


def project(features, norm_gain, kv_weight, heads):
    tokens, width = features.shape
    cols = kv_weight.shape[1] // heads
    blocks = 4
    anywhere = pl.BlockSpec(memory_space=pl.ANY)
    return pl.pallas_call(
        project_kernel,
        in_specs=[anywhere] * 3,
        out_specs=pl.BlockSpec(memory_space=pltpu.VMEM),
        out_shape=jax.ShapeDtypeStruct((heads, tokens + EXTRA, cols), jnp.bfloat16),
        scratch_shapes=[
            pltpu.VMEM((tokens, width), features.dtype),
            pltpu.VMEM((1, width), norm_gain.dtype),
            pltpu.VMEM((blocks, width, kv_weight.shape[1] // blocks), kv_weight.dtype),
            pltpu.SemaphoreType.DMA((blocks + 2,)),
        ],
        compiler_params=pltpu.CompilerParams(vmem_limit_bytes=60 << 20),
        name="project",
    )(features, norm_gain.reshape(1, width), kv_weight)


def reduce_kernel(width, parts, out, work):
    tokens = out.shape[0]
    total = jnp.sum(parts[:, tokens:, :128].astype(jnp.float32), axis=0)
    squares = jnp.broadcast_to(total[0:1] + total[1:2], (128, tokens)).T
    inverse = lax.rsqrt(squares / width + 1e-05)
    for half in range(2):
        cols = slice(half * 128, half * 128 + 128)
        kept = parts[0, :tokens, cols].astype(jnp.float32)
        for s in range(1, parts.shape[0]):
            kept = kept + parts[s, :tokens, cols].astype(jnp.float32)
        kept = (kept * inverse).astype(jnp.bfloat16)
        out[:, cols] = kept
        work[:, cols] = kept


def prepare_kernel(blocks_dev, place, lists, docs, table, seen):
    t = place[0]
    z = t // 4
    low = lax.rem(t, 4)
    units = lists.shape[0]
    d = docs[...]
    starts = [0] + [jnp.sum((d < doc).astype(jnp.int32)) for doc in range(1, DOCS)]
    for doc in range(DOCS):
        table[units * LINE + doc] = starts[doc]
    for c in range(seen.shape[0]):
        seen[c] = -1

    def unit_lists(u, carry):
        block = t * blocks_dev + lax.rem(u, blocks_dev)
        first = block * BLK
        begin = 0
        for doc in range(1, DOCS):
            begin = jnp.where(starts[doc] <= first, starts[doc], begin)
        least = begin // BLK
        base = u * LINE
        for e in range(LIST):
            table[base + e] = 0
            table[base + LIST + e] = FAR
            table[base + 2 * LIST + e] = 0
            table[base + 3 * LIST + e] = FAR
        near = 0
        far = 0
        for e in range(LIST):
            c = lists[u, e]
            keep = (c >= least) & (seen[c] != u)
            seen[c] = u
            away = z - c // 8
            x = lax.rem(c // 2, 4) ^ low
            inner = lax.rem(c, 2) * BLK
            y = x >> 1
            core = x & 1
            is_near = (away <= 1) | (y == 0) | (away >= 5)
            near_row = jnp.where(
                away <= 1,
                y * (CLOSE // 2) + away * CHUNK,
                jnp.where(away <= 4, CLOSE + (away - 2) * CHUNK, CLOSE + RISING + y * FALLING + (6 - away) * CHUNK),
            )
            near_row += core * NEAR_ROWS + inner
            far_row = core * FAR_ROWS + (away - 2) * CHUNK + inner
            at = base + jnp.where(is_near, near, 2 * LIST + far)
            row = jnp.where(is_near, near_row, far_row)
            table[at] = jnp.where(keep, row, 0)
            table[at + LIST] = jnp.where(keep, c * BLK, FAR)
            near = near + (keep & is_near).astype(jnp.int32)
            far = far + (keep & ~is_near).astype(jnp.int32)
        counts = units * LINE + COUNTS + u
        table[counts] = near
        table[counts + units] = far
        return carry

    lax.fori_loop(0, units, unit_lists, 0)


def scores(blocks, base, block, extra, begins, table, queries, held):
    pieces = [held[pl.ds(pl.multiple_of(table[base + e], BLK), BLK), :] for e in range(blocks)]
    pieces += [rows for rows, _ in extra]
    kv = jnp.concatenate(pieces, axis=0)
    lane = lax.rem(lax.broadcasted_iota(jnp.int32, (1, 128), 1), BLK)
    sub = lax.broadcasted_iota(jnp.int32, (BLK, 128), 0)
    pos_i = block * BLK + lane
    masks = []
    for e in range(blocks):
        pos_j = table[base + LIST + e] + sub
        masks.append((pos_j >= begins) & (pos_j <= pos_i))
    masks += [(sub == lane) & allowed for _, allowed in extra]
    mask = jnp.concatenate(masks, axis=0)
    mask = jnp.concatenate([mask] * (queries.shape[0] // 128), axis=1)
    s = lax.dot_general(kv[:, :HEAD], queries, (((1,), (1,)), ((), ())), preferred_element_type=jnp.float32)
    return jnp.where(mask, s, HIDDEN), kv[:, HEAD:]


def weigh(p, values):
    return lax.dot_general(
        values, p.astype(jnp.bfloat16), (((0,), (0,)), ((), ())), preferred_element_type=jnp.float32
    )


def unit_state(blocks_dev, u, t, table, q):
    steps, heads, tokens, head_dim = q.shape
    units = steps * blocks_dev
    k = u // blocks_dev
    half = lax.rem(u, blocks_dev)
    block = t * blocks_dev + half
    rows = pl.ds(pl.multiple_of(half * BLK, BLK), BLK)
    queries = q[k, :, rows, :].reshape(heads * BLK, head_dim)
    pos_i = block * BLK + lax.rem(lax.broadcasted_iota(jnp.int32, (1, 128), 1), BLK)
    begins = jnp.zeros((1, 128), jnp.int32)
    for doc in range(1, DOCS):
        start = table[units * LINE + doc]
        begins = jnp.where(start <= pos_i, start, begins)
    return k, block, rows, queries, begins


def per_size(sizes, n, run):
    least = -1
    for size in sizes:
        pl.when((n > least) & (n <= size))(functools.partial(run, size))
        least = size


SCALE = math.log2(math.e) / math.sqrt(HEAD)


def hold(held, parts):
    row = 0
    for part in parts:
        held[row : row + part.shape[0]] = part[...]
        row += part.shape[0]


def own_kernel(blocks_dev, q, own, state, sums):
    steps, heads, tokens, head_dim = q.shape

    def body(u, carry):
        k = u // blocks_dev
        rows = pl.ds(pl.multiple_of(lax.rem(u, blocks_dev) * BLK, BLK), BLK)
        queries = q[k, :, rows, :].reshape(heads * BLK, head_dim)
        extra = [(own[m, 0, rows, :], m <= k) for m in range(steps)]
        s, values = scores(0, 0, 0, extra, None, None, queries, None)
        top = jnp.max(s, axis=0, keepdims=True)
        p = jnp.exp2((s - top) * SCALE)
        sums[u, 0:1] = top
        sums[u, 1:2] = jnp.sum(p, axis=0, keepdims=True)
        state[u] = weigh(p, values)
        return carry

    lax.fori_loop(0, steps * blocks_dev, body, 0)


def add_blocks(size, u, base, block, begins, table, queries, held, state, sums):
    top, total, summed = sums[u, 0:1], sums[u, 1:2], state[u]
    if size:
        s, values = scores(size, base, block, [], begins, table, queries, held)
        new_top = jnp.maximum(top, jnp.max(s, axis=0, keepdims=True))
        p = jnp.exp2((s - new_top) * SCALE)
        factor = jnp.exp2((top - new_top) * SCALE)
        total = total * factor + jnp.sum(p, axis=0, keepdims=True)
        summed = summed * factor + weigh(p, values)
        top = new_top
    return top, total, summed


def near_kernel(blocks_dev, place, table, q, old_state, old_sums, mine, theirs, state, sums, held):
    t = place[0]
    units = q.shape[0] * blocks_dev
    hold(held, (mine, theirs))

    def body(u, carry):
        k, block, rows, queries, begins = unit_state(blocks_dev, u, t, table, q)

        def run(size):
            top, total, summed = add_blocks(
                size, u, u * LINE, block, begins, table, queries, held, old_state, old_sums
            )
            sums[u, 0:1] = top
            sums[u, 1:2] = total
            state[u] = summed

        per_size(NEAR_SIZES, table[units * LINE + COUNTS + u], run)
        return carry

    lax.fori_loop(0, units, body, 0)


def far_kernel(blocks_dev, place, table, q, state, sums, mine, theirs, out, held, result, sems):
    t = place[0]
    steps, heads, tokens, head_dim = q.shape
    units = steps * blocks_dev
    hold(held, (mine, theirs))

    def copy(u):
        rows = pl.ds(pl.multiple_of(lax.rem(u, blocks_dev) * BLK, BLK), BLK)
        return pltpu.make_async_copy(result.at[u], out.at[u // blocks_dev, :, rows, :], sems.at[u])

    def body(u, carry):
        k, block, rows, queries, begins = unit_state(blocks_dev, u, t, table, q)

        def run(size):
            top, total, summed = add_blocks(
                size, u, u * LINE + 2 * LIST, block, begins, table, queries, held, state, sums
            )
            result[u] = (summed * (1.0 / total)).T.astype(jnp.bfloat16).reshape(heads, BLK, head_dim)

        per_size(FAR_SIZES, table[units * LINE + COUNTS + units + u], run)
        copy(u).start()
        return carry

    lax.fori_loop(0, units, body, 0)
    lax.fori_loop(0, units, lambda u, c: (copy(u).wait(), c)[1], 0)


SMEM_ALL = pl.BlockSpec(memory_space=pltpu.SMEM)
VMEM_WHOLE = pl.BlockSpec(memory_space=pltpu.VMEM)


def limit(mib):
    return pltpu.CompilerParams(vmem_limit_bytes=mib << 20)


def state_shapes(queries, blocks_dev):
    steps, heads, tokens, head_dim = queries.shape
    units = steps * blocks_dev
    return [
        jax.ShapeDtypeStruct((units, head_dim, heads * BLK), jnp.float32),
        jax.ShapeDtypeStruct((units, 8, heads * BLK), jnp.float32),
    ]


def attend_own(queries, step_kv, blocks_dev):
    return pl.pallas_call(
        functools.partial(own_kernel, blocks_dev),
        in_specs=[VMEM_WHOLE] * 2,
        out_specs=[VMEM_WHOLE] * 2,
        out_shape=state_shapes(queries, blocks_dev),
        compiler_params=limit(16),
        name="attend_own",
    )(queries, step_kv)


def attend_near(place, table, queries, state, sums, mine, theirs, blocks_dev):
    return pl.pallas_call(
        functools.partial(near_kernel, blocks_dev),
        in_specs=[SMEM_ALL] * 2 + [VMEM_WHOLE] * 5,
        out_specs=[VMEM_WHOLE] * 2,
        out_shape=state_shapes(queries, blocks_dev),
        input_output_aliases={3: 0, 4: 1},
        scratch_shapes=[pltpu.VMEM((2 * NEAR_ROWS, mine.shape[1]), jnp.bfloat16)],
        compiler_params=limit(24),
        name="attend_near",
    )(place, table, queries, state, sums, mine, theirs)


def attend_far(place, table, queries, state, sums, mine, theirs, blocks_dev):
    steps, heads, tokens, head_dim = queries.shape
    units = steps * blocks_dev
    return pl.pallas_call(
        functools.partial(far_kernel, blocks_dev),
        in_specs=[SMEM_ALL, SMEM_ALL] + [VMEM_WHOLE] * 5,
        out_specs=pl.BlockSpec(memory_space=pl.ANY),
        out_shape=jax.ShapeDtypeStruct(queries.shape, jnp.bfloat16),
        scratch_shapes=[
            pltpu.VMEM((2 * FAR_ROWS, 2 * head_dim), jnp.bfloat16),
            pltpu.VMEM((units, heads, BLK, head_dim), jnp.bfloat16),
            pltpu.SemaphoreType.DMA((units,)),
        ],
        compiler_params=limit(24),
        name="attend_far",
    )(place, table, queries, state, sums, mine, theirs)


def per_device(features, norm_gain, kv_weight, queries, step_kv, doc_ids, block_lists):
    sections = lax.axis_size("section")
    seqs = lax.axis_size("seq")
    step_total, local_heads, tok_dev, head_dim = queries.shape
    blocks_dev = tok_dev // BLK
    units = step_total * blocks_dev
    place = lax.axis_index("seq").reshape(1).astype(jnp.int32)

    partial = project(features, norm_gain, kv_weight, sections)
    parts = lax.all_to_all(partial, "section", 0, 0, tiled=True)
    lists = lax.dynamic_slice_in_dim(block_lists, place[0] * blocks_dev, blocks_dev, 1).reshape(units, LIST)
    table = pl.pallas_call(
        functools.partial(prepare_kernel, blocks_dev),
        in_specs=[SMEM_ALL, SMEM_ALL, VMEM_WHOLE],
        out_specs=SMEM_ALL,
        out_shape=jax.ShapeDtypeStruct(((units + 1) * LINE,), jnp.int32),
        scratch_shapes=[pltpu.SMEM((block_lists.shape[1],), jnp.int32)],
        compiler_params=limit(4),
        name="prepare",
    )(place, lists, doc_ids.reshape(-1, 128))

    state, sums = attend_own(queries, step_kv, blocks_dev)
    parts, table, state, sums = lax.optimization_barrier((parts, table, state, sums))
    kv_cache, kv = pl.pallas_call(
        functools.partial(reduce_kernel, float(features.shape[1] * sections)),
        out_shape=[jax.ShapeDtypeStruct((tok_dev, 2 * head_dim), jnp.bfloat16)] * 2,
        compiler_params=limit(8),
        name="reduce",
    )(parts)

    every = range(seqs)

    def along_z(x, levels):
        return lax.ppermute(x, "seq", [(i, (i + 4 * levels) % seqs) for i in every])

    def along_y(x):
        return lax.ppermute(x, "seq", [(i, i ^ 2) for i in every])

    def along_core(x):
        return lax.ppermute(x, "seq", [(i, i ^ 1) for i in every])

    def join(*arrays):
        return jnp.concatenate(arrays, axis=0)

    moves = [(4 * z + i, (4 * z - 4) % seqs + i) for z in range(3) for i in range(4)]
    down1 = lax.ppermute(kv, "seq", moves)
    up1 = along_z(kv, 1)
    high, low = lax.optimization_barrier((join(kv, down1), join(kv, up1)))
    down23 = along_z(high, -2)
    up23 = along_z(low, 2)
    low_y = along_y(low)
    up4 = along_z(low[:tok_dev], 4)
    falling = join(down23, along_y(down23))
    rising = join(up23, up4)
    far = along_y(rising)
    near = join(low, low_y, rising, falling)
    state, sums = attend_near(place, table, queries, state, sums, near, along_core(near), blocks_dev)
    far, state, sums = lax.optimization_barrier((far, state, sums))
    attended = attend_far(place, table, queries, state, sums, far, along_core(far), blocks_dev)
    return attended, kv_cache[None]


def solution(mesh):
    in_specs = (
        P("seq", "section"),
        P("section"),
        P("section", None),
        P(None, "section", "seq", None),
        P(None, "section", "seq", None),
        P(),
        P(),
    )
    out_specs = (P(None, "section", "seq", None), P("section", "seq", None))
    return jax.shard_map(per_device, mesh=mesh, in_specs=in_specs, out_specs=out_specs, check_vma=False)
```
